512 devices in a mesh: gx: 16 (over z_lo, x), yz: 32 (over z_hi, y, core).
Axes of the slice: x: 4, y: 4, z: 16 (z_hi: 4, z_lo: 4; z = z_hi * 4 + z_lo), core: 2. Of those that a mesh axis runs over, the one named last changes fastest.
Arguments:
- nodes: float32 [3, 2097152], P(None, ('gx', 'yz')), may hold values from -4 to 4
- links: int32 [2, 2097152], P(None, ('gx', 'yz')), may hold values from 0 to 4095, as said below
- burgers: float32 [3, 2097152], P(None, ('gx', 'yz')), may hold values from -4 to 4
- mobility: float32 [3, 3, 2097152], P(None, None, ('gx', 'yz'))
- send_list: int32 [512, 8, 6], P(('gx', 'yz')), may hold values from 0 to 31
- pair_list: int32 [2, 81920], P(None, ('gx', 'yz')), may hold values from 0 to 79, as said below
- pair_count: int32 [512], P(('gx', 'yz')), may hold values from 48 to 160, as said below
Outputs:
- displacement: float32 [3, 2097152], P(None, ('gx', 'yz'))
The draws below stay inside these ranges and needn't reach their ends.
Inputs may be any that keep to these rules, and one draw needn't show every extreme that they name: Within each domain the links form one closed loop: every node of the domain ends exactly two of its segments; entries are node numbers within the domain. `pair_list`: row 0 holds target block numbers below 32; row 1 holds source numbers; every ghost slot of a domain is named by one of its live entries; entries at or past the domain's pair_count are unused. `pair_count`: the largest count equals 160 in every draw.
All inputs are finite; a program needn't handle non-finite values.
Results may differ from the reference program's by a relative error of at most 0.0003.
Values sent between devices are 32-bit elements; how exact they have to be, the bound alone decides.
A program may use at most 64 MiB of HBM per device.

```python
import math
import jax
import jax.numpy as jnp
from jax import lax

BLK_DEV = 32
GB = 6
PAIRS = 160
DOMAINS = 512
SEG_DEV = 4096
SEGS = 2097152
NODES = 2097152
N_GX = 16
N_YZ = 32


def pair_tables(key):
    keys = jax.random.split(jax.random.fold_in(key, 11), 5)
    ghost_slots = 8 * GB
    levels = jax.random.randint(keys[0], (DOMAINS,), 0, 16)
    busiest = jax.random.randint(keys[1], (), 0, DOMAINS)
    levels = jnp.where(jnp.arange(DOMAINS) == busiest, 15, levels)
    counts = ghost_slots + (PAIRS - ghost_slots) * levels * levels // 225
    targets = jax.random.randint(keys[2], (DOMAINS, PAIRS), 0, BLK_DEV)
    others = jax.random.randint(keys[3], (DOMAINS, PAIRS), 0, BLK_DEV + ghost_slots)
    orders = jax.vmap(lambda one_key: jax.random.permutation(one_key, ghost_slots))(jax.random.split(keys[4], DOMAINS))
    padded_orders = jnp.concatenate([orders, jnp.zeros((DOMAINS, PAIRS - ghost_slots), jnp.int32)], axis=1)
    position = jnp.arange(PAIRS)[None, :]
    sources = jnp.where(position < ghost_slots, BLK_DEV + padded_orders, others)
    table = jnp.stack([targets, sources]).reshape(2, DOMAINS * PAIRS)
    return (table.astype(jnp.int32), counts.astype(jnp.int32))


def draw_pair_list(key, part):
    return pair_tables(key)[0]


def draw_pair_count(key, part):
    return pair_tables(key)[1]


def draw_links(key, part):
    keys = jax.random.split(jax.random.fold_in(key, 5), DOMAINS)
    orders = jax.vmap(lambda one_key: jax.random.permutation(one_key, SEG_DEV))(keys)
    return jnp.stack([orders, jnp.roll(orders, -1, axis=1)]).reshape(2, DOMAINS * SEG_DEV).astype(jnp.int32)


def draw_mobility(key, part):
    keys = jax.random.split(jax.random.fold_in(key, 3), 3)
    diagonal = jax.random.uniform(keys[0], (3, NODES), minval=0.5, maxval=1.5)
    offdiag = jax.random.uniform(keys[1], (3, NODES), minval=-0.2, maxval=0.2)
    domain = (jnp.arange(NODES) // SEG_DEV).astype(jnp.float32)
    rising = 1.0 + 2.0 * domain / max(DOMAINS - 1, 1)
    scales = jnp.exp(jax.random.uniform(keys[2], (NODES,), minval=0.0, maxval=math.log(2.0)))
    factor = rising * scales
    first_row = jnp.stack([diagonal[0], offdiag[0], offdiag[1]])
    second_row = jnp.stack([offdiag[0], diagonal[1], offdiag[2]])
    third_row = jnp.stack([offdiag[1], offdiag[2], diagonal[2]])
    return (jnp.stack([first_row, second_row, third_row]) * factor).astype(jnp.float32)


def set_ends(entries, rng, smallest, top_value):
    index_at = [jax.random.randint(jax.random.fold_in(rng, axis), (), 0, length) for axis, length in enumerate(entries.shape)]
    widest = entries.shape.index(max(entries.shape))
    beside = index_at[:widest] + [(index_at[widest] + 1) % entries.shape[widest]] + index_at[widest + 1:]
    return entries.at[tuple(index_at)].set(smallest).at[tuple(beside)].set(top_value)


def steps_of(stream_key, shape, cuts, least, largest):
    def one(dim, shards_of):
        heights = jax.random.uniform(jax.random.fold_in(jax.random.fold_in(stream_key, 6), dim), (shards_of,), jnp.float32, least / len(cuts), largest / len(cuts))
        return jnp.repeat(jnp.exp(heights), shape[dim] // shards_of).reshape((-1,) + (1,) * (len(shape) - dim - 1))

    factor_of = one(*cuts[0])
    for cut in cuts[1:]:
        factor_of = factor_of * one(*cut)
    return factor_of


def scatter_about(stream_key, extent, scale, bound, cuts=(), held_as=jnp.bfloat16):
    values = scale * jax.random.normal(stream_key, extent, jnp.float32)
    if cuts:
        values = values * steps_of(stream_key, extent, cuts, -0.22, 0.18)
    return jnp.clip(values, -bound, bound).astype(held_as)


def setup_inputs(seed: int = 0) -> dict:
    key_of = jax.random.split(jax.random.key(seed), 8)
    return {
        "nodes": scatter_about(key_of[0], (3, NODES), 1.0, 4.0, ((1, 512),), jnp.float32),
        "links": draw_links(jax.random.fold_in(key_of[7], 71), 0),
        "burgers": scatter_about(key_of[2], (3, SEGS), 1.0, 4.0, ((1, 512),), jnp.float32),
        "mobility": draw_mobility(jax.random.fold_in(key_of[7], 71), 0),
        "send_list": set_ends(jax.random.randint(key_of[4], (DOMAINS, 8, GB), 0, BLK_DEV), jax.random.fold_in(key_of[4], 1), 0, BLK_DEV - 1).astype(jnp.int32),
        "pair_list": draw_pair_list(jax.random.fold_in(key_of[7], 71), 0),
        "pair_count": draw_pair_count(jax.random.fold_in(key_of[7], 71), 0),
    }


A_SQUARED = 0.25
NU_FACTOR = 0.4
DX_LIMIT = 1.0
SPEED_EPS = 1e-05
DIRECTIONS = ((-1, -1), (-1, 0), (-1, 1), (0, -1), (0, 1), (1, -1), (1, 0), (1, 1))

def crossed(left, right):
    return jnp.stack([left[1] * right[2] - left[2] * right[1], left[2] * right[0] - left[0] * right[2], left[0] * right[1] - left[1] * right[0]])

def make_blocks(points, links, burgers):
    first = jnp.take(points, links[0], axis=1)
    second = jnp.take(points, links[1], axis=1)
    data = jnp.concatenate([0.5 * (first + second), second - first, burgers], axis=0)
    return data.reshape(9, -1, 128).transpose(1, 0, 2)

def tile_traction(target, source):
    relative = target[0:3, :, None] - source[0:3, None, :]
    distance = lax.optimization_barrier(jnp.sum(relative * relative, axis=0)) + A_SQUARED
    inv_cube = 1.0 / (distance * jnp.sqrt(distance))
    line_src = source[3:6, None, :]
    burg_src = source[6:9, None, :]
    burg_tgt = target[6:9, :, None]
    across = crossed(burg_src, relative)
    twisted = lax.optimization_barrier(jnp.sum(burg_src * crossed(line_src, relative), axis=0))
    along = lax.optimization_barrier(jnp.sum(across * burg_tgt, axis=0))
    lined = lax.optimization_barrier(jnp.sum(line_src * burg_tgt, axis=0))
    weight_line = 0.5 * inv_cube * along
    weight_cross = 0.5 * inv_cube * lined
    weight_self = NU_FACTOR * inv_cube * twisted
    return lax.optimization_barrier(jnp.sum(weight_line[None] * line_src, axis=2)) + lax.optimization_barrier(jnp.sum(weight_cross[None] * across, axis=2)) + burg_tgt[:, :, 0] * lax.optimization_barrier(jnp.sum(weight_self, axis=1))[None]

def nodal_velocity(traction, blocks, links, mobility):
    seg_count = links.shape[1]
    traction_rows = traction.transpose(1, 0, 2).reshape(3, seg_count)
    line_rows = blocks[:, 3:6].transpose(1, 0, 2).reshape(3, seg_count)
    half_force = 0.5 * crossed(traction_rows, line_rows)
    nodal = jnp.zeros((3, mobility.shape[2]), jnp.float32)
    nodal = nodal.at[:, links[0]].add(half_force).at[:, links[1]].add(half_force)
    return lax.optimization_barrier(jnp.sum(mobility * nodal[None], axis=1))

def domain_velocity(operands):
    links, mobility, blocks, ghosts, pair_rows, live_count = operands
    sources = jnp.concatenate([blocks, ghosts], axis=0)
    tile_terms = jax.vmap(tile_traction)(blocks[pair_rows[0]], sources[pair_rows[1]])
    live_mask = jnp.arange(pair_rows.shape[1]) < live_count
    tile_terms = jnp.where(live_mask[:, None, None], tile_terms, 0.0)
    traction = jnp.zeros((blocks.shape[0], 3, 128), jnp.float32).at[pair_rows[0]].add(tile_terms)
    return nodal_velocity(traction, blocks, links, mobility)

def reference(nodes, links, burgers, mobility, send_list, pair_list, pair_count):
    domain_total = N_GX * N_YZ
    seg_count = links.shape[1] // domain_total
    links_dom = links.reshape(2, domain_total, seg_count).transpose(1, 0, 2)
    burg_dom = burgers.reshape(3, domain_total, seg_count).transpose(1, 0, 2)
    mob_dom = mobility.reshape(3, 3, domain_total, seg_count).transpose(2, 0, 1, 3)
    pairs_dom = pair_list.reshape(2, domain_total, -1).transpose(1, 0, 2)
    shift_gx = jnp.array([item[0] for item in DIRECTIONS], jnp.int32)
    shift_yz = jnp.array([item[1] for item in DIRECTIONS], jnp.int32)
    domain_ids = jnp.arange(domain_total, dtype=jnp.int32)
    row_gx = domain_ids // N_YZ
    row_yz = domain_ids % N_YZ
    anchor = (row_gx[:, None] - shift_gx[None]) % N_GX * N_YZ + (row_yz[:, None] - shift_yz[None]) % N_YZ
    slots = jnp.arange(8, dtype=jnp.int32)[None, :]

    def evaluate(points):
        pts_dom = points.reshape(3, domain_total, seg_count).transpose(1, 0, 2)
        blocks = jax.vmap(make_blocks)(pts_dom, links_dom, burg_dom)
        outgoing = jax.vmap(lambda block_set, chosen: block_set[chosen])(blocks, send_list)
        ghosts = outgoing[anchor, slots]
        ghosts = ghosts.reshape(domain_total, -1, 9, 128)
        speeds = lax.map(domain_velocity, (links_dom, mob_dom, blocks, ghosts, pairs_dom, pair_count))
        return speeds.transpose(1, 0, 2).reshape(3, -1)
    first_speed = evaluate(nodes)
    global_top = jnp.max(jnp.sqrt(lax.optimization_barrier(jnp.sum(first_speed * first_speed, axis=0))))
    step_size = DX_LIMIT / (global_top + SPEED_EPS)
    second_speed = evaluate(nodes + step_size * first_speed)
    return 0.5 * step_size * (first_speed + second_speed)
```

```python
import functools

import jax
import jax.numpy as jnp
from jax import lax
from jax.experimental import pallas as pl
from jax.experimental.pallas import tpu as pltpu
from jax.sharding import PartitionSpec as P

F32 = jnp.float32
BF16 = jnp.bfloat16
A_SQUARED = 0.25
NU_FACTOR = 0.4
DX_LIMIT = 1.0
SPEED_EPS = 1e-05
DIRECTIONS = ((-1, -1), (-1, 0), (-1, 1), (0, -1), (0, 1), (1, -1), (1, 0), (1, 1))
BLK = 32
LANE = 128
GB = 6
SLOTS = BLK + 64
QROWS = 32
FROWS = 40
UNROLL = 4
MESH_ID = pl.DeviceIdType.MESH


def cross(u, v):
    return [u[1] * v[2] - u[2] * v[1], u[2] * v[0] - u[0] * v[2], u[0] * v[1] - u[1] * v[0]]


def dot3(u, v):
    return u[0] * v[0] + u[1] * v[1] + u[2] * v[2]


def rounded(x):
    return x.astype(BF16).astype(F32)


def split2(x):
    high = rounded(x)
    return high, rounded(x - high)


def split3(x):
    high = rounded(x)
    rest = x - high
    mid = rounded(rest)
    return high, mid, rounded(rest - mid)


def to_rows(src_ref, rows, stage_ref, lead=None):
    for k in range(BLK):
        lanes = pl.ds(k * LANE, LANE)
        piece = src_ref[:, lanes] if lead is None else src_ref[lead, :, lanes]
        stage_ref[8 * k : 8 * k + rows, :] = piece
    return [stage_ref[pl.ds(c, BLK, stride=8), :] for c in range(rows)]


def gather_ends(table_ref, ends):
    outs = []
    for end in ends:
        high = end >> 7
        low = end & 127
        picked = [jnp.zeros((BLK, LANE), F32) for _ in range(3)]
        for row in range(BLK):
            here = high == row
            for c in range(3):
                wide = jnp.broadcast_to(table_ref[c, row : row + 1, :], (BLK, LANE))
                found = jnp.take_along_axis(wide, low, axis=1, mode="promise_in_bounds")
                picked[c] = jnp.where(here, found, picked[c])
        outs.append(picked)
    return outs


def pack_blocks(send_list, block_ref, rows, send_ref):
    for k in range(8):
        for g in range(GB):
            chosen = send_list[0, k, g]
            send_ref[k, rows * g : rows * (g + 1), :] = block_ref[chosen, 0:rows, :]


def prepare_kernel(send_list, nodes_ref, links_ref, burgers_ref, own_ref, ends_ref, send_ref, stage_ref, table_ref, block_ref):
    coords = to_rows(nodes_ref, 3, stage_ref)
    for c in range(3):
        table_ref[c] = coords[c]
    for k in range(BLK):
        lanes = pl.ds(k * LANE, LANE)
        ends_ref[0, k : k + 1, :] = links_ref[0:1, lanes]
        ends_ref[1, k : k + 1, :] = links_ref[1:2, lanes]
    first, second = gather_ends(table_ref, [ends_ref[0], ends_ref[1]])
    burgers = to_rows(burgers_ref, 3, stage_ref)
    rows = [0.5 * (first[c] + second[c]) for c in range(3)] + [second[c] - first[c] for c in range(3)] + burgers
    for c in range(9):
        own_ref[c] = rows[c]
        for k in range(BLK):
            block_ref[k, c : c + 1, :] = rows[c][k : k + 1]
    pack_blocks(send_list, block_ref, 9, send_ref)


def neighbours():
    gx = lax.axis_index("gx")
    yz = lax.axis_index("yz")
    n_gx = lax.axis_size("gx")
    n_yz = lax.axis_size("yz")
    return [(lax.rem(gx + dx + n_gx, n_gx), lax.rem(yz + dy + n_yz, n_yz)) for dx, dy in DIRECTIONS]


def greet(targets):
    barrier = pltpu.get_barrier_semaphore()
    for target in targets:
        pl.semaphore_signal(barrier, inc=1, device_id=target, device_id_type=MESH_ID)
    pl.semaphore_wait(barrier, len(targets))


def ghost_copies(send_ref, recv_ref, send_sem, recv_sem, targets):
    return [
        pltpu.make_async_remote_copy(
            src_ref=send_ref.at[k],
            dst_ref=recv_ref.at[k],
            send_sem=send_sem.at[k],
            recv_sem=recv_sem.at[k],
            device_id=targets[k],
            device_id_type=MESH_ID,
        )
        for k in range(8)
    ]


def exchange_kernel(send_ref, recv_ref, send_sem, recv_sem):
    targets = neighbours()
    greet(targets)
    copies = ghost_copies(send_ref, recv_ref, send_sem, recv_sem, targets)
    for copy in copies:
        copy.start()
    for copy in copies:
        copy.wait()


def exchange_max_kernel(n_gx, n_yz, send_ref, top_ref, recv_ref, out_ref, box_gx, box_yz, mid_ref, send_sem, recv_sem, sgx, rgx, syz, ryz):
    targets = neighbours()
    gx = lax.axis_index("gx")
    yz = lax.axis_index("yz")
    line_gx = [(lax.rem(gx + o, n_gx), yz) for o in range(1, n_gx)]
    line_yz = [(gx, lax.rem(yz + o, n_yz)) for o in range(1, n_yz)]
    corners = [targets[k] for k in (0, 2, 5, 7)]
    greet(line_gx + line_yz + corners)

    def spread(source, box, send, recv, line):
        return [
            pltpu.make_async_remote_copy(
                src_ref=source,
                dst_ref=box.at[o + 1],
                send_sem=send.at[o + 1],
                recv_sem=recv.at[o + 1],
                device_id=line[o],
                device_id_type=MESH_ID,
            )
            for o in range(len(line))
        ]

    along_gx = spread(top_ref, box_gx, sgx, rgx, line_gx)
    for copy in along_gx:
        copy.start()
    copies = ghost_copies(send_ref, recv_ref, send_sem, recv_sem, targets)
    for copy in copies:
        copy.start()
    best = top_ref[...]
    for copy in along_gx:
        copy.wait_recv()
    for o in range(1, n_gx):
        best = jnp.maximum(best, box_gx[o])
    mid_ref[...] = best
    along_yz = spread(mid_ref, box_yz, syz, ryz, line_yz)
    for copy in along_yz:
        copy.start()
    for copy in along_yz:
        copy.wait_recv()
    for o in range(1, n_yz):
        best = jnp.maximum(best, box_yz[o])
    out_ref[...] = best
    for copy in along_gx:
        copy.wait_send()
    for copy in along_yz:
        copy.wait_send()
    for copy in copies:
        copy.wait()


def source_features(mid, line, burg, slot, qs_ref, f_ref):
    def put_q(row, value):
        qs_ref[pl.ds(slot * QROWS + row, BLK, stride=QROWS), :] = value

    def put_f(row, value):
        f_ref[pl.ds(slot * FROWS + row, BLK, stride=FROWS), :] = value

    row = 0
    for c in range(3):
        high, middle, low = split3(mid[c])
        for part in (high, high, middle, middle, high, low):
            put_q(row, part)
            row += 1
    for part in split3(dot3(mid, mid) + A_SQUARED):
        put_q(row, part)
        row += 1
    one = jnp.ones((BLK, LANE), F32)
    zero = jnp.zeros((BLK, LANE), F32)
    for _ in range(3):
        put_q(row, one)
        row += 1
    while row < QROWS:
        put_q(row, zero)
        row += 1
    moment = cross(burg, mid)
    for a in range(3):
        for d in range(3):
            high, low = split2(line[a] * burg[d])
            put_f(3 * a + d, high)
            put_f(18 + 3 * a + d, low)
            high, low = split2(line[a] * moment[d])
            put_f(9 + 3 * a + d, high)
            put_f(27 + 3 * a + d, low)


def target_features(mid, qt_ref):
    def put(row, value):
        qt_ref[pl.ds(row, BLK, stride=QROWS), :] = value

    row = 0
    for c in range(3):
        high, middle, low = split3(-2.0 * mid[c])
        for part in (high, middle, high, middle, low, high):
            put(row, part)
            row += 1
    one = jnp.ones((BLK, LANE), F32)
    zero = jnp.zeros((BLK, LANE), F32)
    for _ in range(3):
        put(row, one)
        row += 1
    for part in split3(dot3(mid, mid)):
        put(row, part)
        row += 1
    while row < QROWS:
        put(row, zero)
        row += 1


def velocity(own, ghost, pairs, count, ends_ref, mob_ref, scr):
    qs_f, qt_f, f_f, qs_b, qt_b, f_b, acc, force_ref = scr
    centre = [jnp.mean(own[c]) for c in range(3)]
    mid = [own[c] - centre[c] for c in range(3)]
    line = own[3:6]
    burg = own[6:9]
    source_features(mid, line, burg, 0, qs_f, f_f)
    target_features(mid, qt_f)
    for half in range(2):
        rows = [ghost(c, half) for c in range(9)]
        source_features([rows[c] - centre[c] for c in range(3)], rows[3:6], rows[6:9], BLK * (half + 1), qs_f, f_f)

    def convert(step, carry):
        for j in range(4):
            slot = 4 * step + j
            q = qs_f[pl.ds(pl.multiple_of(slot * QROWS, 8), QROWS), :]
            qs_b[slot] = jnp.transpose(q).astype(BF16)
            f = f_f[pl.ds(pl.multiple_of(slot * FROWS, 8), FROWS), :].astype(BF16)
            f_b[slot] = jnp.concatenate([f, f], axis=1)
        return carry

    lax.fori_loop(0, SLOTS // 4, convert, 0)

    def convert_target(step, carry):
        for j in range(4):
            slot = 4 * step + j
            qt_b[slot] = qt_f[pl.ds(pl.multiple_of(slot * QROWS, 8), QROWS), :].astype(BF16)
        return carry

    lax.fori_loop(0, BLK // 4, convert_target, 0)
    acc[...] = jnp.zeros(acc.shape, F32)

    def pair_step(step, carry):
        found = []
        for j in range(UNROLL):
            place = UNROLL * step + j
            live = place < count
            target = jnp.where(live, pairs[0, place], BLK)
            source = jnp.where(live, pairs[1, place], 0)
            ghost_place = source - BLK
            group = (ghost_place * 43) >> 8
            slot = jnp.where(source < BLK, source, BLK + 8 * group + (ghost_place - GB * group))
            dist = jnp.dot(qs_b[slot], qt_b[target], preferred_element_type=F32)
            root = lax.rsqrt(dist)
            weight = root * root * root
            high = weight.astype(BF16)
            low = (weight - high.astype(F32)).astype(BF16)
            both = jnp.concatenate([high, low], axis=0)
            found.append((target, jnp.dot(f_b[slot], both, preferred_element_type=F32)))
        for target, part in found:
            acc[target] += part
        return carry

    lax.fori_loop(0, (count + UNROLL - 1) // UNROLL, pair_step, 0)

    def total(row):
        return acc[0:BLK, row, :] + acc[0:BLK, row + 18, :]

    s_mat = [[total(3 * a + d) for d in range(3)] for a in range(3)]
    t_mat = [[total(9 + 3 * a + d) for d in range(3)] for a in range(3)]
    arm = cross(mid, burg)
    lined_s = [burg[0] * s_mat[0][d] + burg[1] * s_mat[1][d] + burg[2] * s_mat[2][d] for d in range(3)]
    lined_t = [burg[0] * t_mat[0][d] + burg[1] * t_mat[1][d] + burg[2] * t_mat[2][d] for d in range(3)]
    swept = cross(lined_s, mid)
    skew = [s_mat[2][1] - s_mat[1][2], s_mat[0][2] - s_mat[2][0], s_mat[1][0] - s_mat[0][1]]
    twist = NU_FACTOR * (dot3(mid, skew) + (t_mat[0][0] + t_mat[1][1] + t_mat[2][2]))
    traction = [
        0.5 * ((dot3(s_mat[k], arm) - dot3(t_mat[k], burg)) + (swept[k] - lined_t[k])) + twist * burg[k]
        for k in range(3)
    ]
    force = cross(traction, line)
    for c in range(3):
        high, low = split2(0.5 * force[c])
        force_ref[2 * c] = high
        force_ref[2 * c + 1] = low

    row_id = lax.broadcasted_iota(jnp.int32, (BLK, LANE), 0)
    lane_id = lax.broadcasted_iota(jnp.int32, (LANE, LANE), 0)

    def scatter_step(k, nodal):
        lhs = []
        rhs = []
        for e in range(2):
            end = ends_ref[e, pl.ds(k, 1), :]
            here = row_id == (end >> 7)
            lhs.append(
                jnp.concatenate(
                    [jnp.where(here, force_ref[i, pl.ds(k, 1), :], 0.0).astype(BF16) for i in range(6)], axis=0
                )
            )
            rhs.append(jnp.where(lane_id == (end & 127), 1.0, 0.0).astype(BF16))
        return nodal + lax.dot_general(
            jnp.concatenate(lhs, axis=1),
            jnp.concatenate(rhs, axis=1),
            (((1,), (1,)), ((), ())),
            preferred_element_type=F32,
        )

    nodal = lax.fori_loop(0, BLK, scatter_step, jnp.zeros((6 * BLK, LANE), F32))
    pulled = [nodal[2 * BLK * c : 2 * BLK * c + BLK] + nodal[2 * BLK * c + BLK : 2 * BLK * (c + 1)] for c in range(3)]
    return [dot3([mob_ref[3 * r + c] for c in range(3)], pulled) for r in range(3)]


def first_kernel(
    send_list, pairs, count, own_ref, recv_ref, ends_ref, mobility_ref,
    v_ref, top_ref, own_v_ref, send_ref, ghost_ref, mob_ref, stage_ref, block_ref, *scr
):
    for r in range(3):
        rows = to_rows(mobility_ref, 3, stage_ref, r)
        for c in range(3):
            mob_ref[3 * r + c] = rows[c]
    for c in range(9):
        for k in range(8):
            ghost_ref[c, 8 * k : 8 * k + GB, :] = recv_ref[k, pl.ds(c, GB, stride=9), :]
            ghost_ref[c, 8 * k + GB : 8 * k + 8, :] = jnp.zeros((8 - GB, LANE), F32)
    own = [own_ref[c] for c in range(9)]
    speed = velocity(own, lambda c, half: ghost_ref[c, BLK * half : BLK * (half + 1), :], pairs, count[0], ends_ref, mob_ref, scr)
    for c in range(3):
        v_ref[c] = speed[c]
    top_ref[...] = jnp.max(dot3(speed, speed), axis=0, keepdims=True)
    first, second = gather_ends(v_ref, [ends_ref[0], ends_ref[1]])
    rows = [0.5 * (first[c] + second[c]) for c in range(3)] + [second[c] - first[c] for c in range(3)]
    for c in range(6):
        own_v_ref[c] = rows[c]
        for k in range(BLK):
            block_ref[k, c : c + 1, :] = rows[c][k : k + 1]
    pack_blocks(send_list, block_ref, 6, send_ref)


def second_kernel(
    pairs, count, own_ref, ghost_ref, own_v_ref, recv_ref, top_ref, v_ref, ends_ref, mob_ref,
    out_ref, moved_ref, stage_ref, *scr
):
    step = DX_LIMIT / (jnp.sqrt(jnp.max(top_ref[...])) + SPEED_EPS)
    for c in range(9):
        if c < 6:
            for k in range(8):
                rows = slice(8 * k, 8 * k + GB)
                moved_ref[c, rows, :] = ghost_ref[c, rows, :] + step * recv_ref[k, pl.ds(c, GB, stride=6), :]
                moved_ref[c, 8 * k + GB : 8 * k + 8, :] = jnp.zeros((8 - GB, LANE), F32)
        else:
            moved_ref[c] = ghost_ref[c]
    own = [own_ref[c] + step * own_v_ref[c] if c < 6 else own_ref[c] for c in range(9)]
    speed = velocity(own, lambda c, half: moved_ref[c, BLK * half : BLK * (half + 1), :], pairs, count[0], ends_ref, mob_ref, scr)
    for c in range(3):
        stage_ref[pl.ds(c, BLK, stride=8), :] = 0.5 * step * (v_ref[c] + speed[c])
    for k in range(BLK):
        out_ref[:, pl.ds(k * LANE, LANE)] = stage_ref[8 * k : 8 * k + 3, :]


VMEM = pl.BlockSpec(memory_space=pltpu.VMEM)
SMEM = pl.BlockSpec(memory_space=pltpu.SMEM)
DMA = pltpu.SemaphoreType.DMA


def shape(*dims, dtype=F32):
    return jax.ShapeDtypeStruct(dims, dtype)


def velocity_scratch():
    return [
        pltpu.VMEM((SLOTS * QROWS, LANE), F32),
        pltpu.VMEM((BLK * QROWS, LANE), F32),
        pltpu.VMEM((SLOTS * FROWS, LANE), F32),
        pltpu.VMEM((SLOTS, LANE, QROWS), BF16),
        pltpu.VMEM((BLK + 1, QROWS, LANE), BF16),
        pltpu.VMEM((SLOTS, FROWS, 2 * LANE), BF16),
        pltpu.VMEM((BLK + 1, FROWS, LANE), F32),
        pltpu.VMEM((6, BLK, LANE), F32),
    ]


STAGE = pltpu.VMEM((BLK * 8, LANE), F32)
BLOCKS = pltpu.VMEM((BLK, 16, LANE), F32)
LOCAL = pltpu.CompilerParams(vmem_limit_bytes=40 * 1024 * 1024)


def prepare(send_list, nodes, links, burgers):
    return pl.pallas_call(
        prepare_kernel,
        out_shape=(shape(9, BLK, LANE), shape(2, BLK, LANE, dtype=jnp.int32), shape(8, 9 * GB, LANE)),
        in_specs=[SMEM, VMEM, VMEM, VMEM],
        out_specs=(VMEM, VMEM, VMEM),
        scratch_shapes=[STAGE, pltpu.VMEM((3, BLK, LANE), F32), BLOCKS],
        compiler_params=LOCAL,
        name="prepare",
    )(send_list, nodes, links, burgers)


def exchange(send):
    return pl.pallas_call(
        exchange_kernel,
        out_shape=shape(*send.shape),
        in_specs=[VMEM],
        out_specs=VMEM,
        scratch_shapes=[DMA((8,)), DMA((8,))],
        compiler_params=pltpu.CompilerParams(collective_id=0, has_side_effects=True, vmem_limit_bytes=4 * 1024 * 1024),
        name="exchange",
    )(send)


def exchange_max(send, top):
    n_gx = lax.axis_size("gx")
    n_yz = lax.axis_size("yz")
    return pl.pallas_call(
        functools.partial(exchange_max_kernel, n_gx, n_yz),
        out_shape=(shape(*send.shape), shape(1, LANE)),
        in_specs=[VMEM, VMEM],
        out_specs=(VMEM, VMEM),
        scratch_shapes=[
            pltpu.VMEM((n_gx, 1, LANE), F32),
            pltpu.VMEM((n_yz, 1, LANE), F32),
            pltpu.VMEM((1, LANE), F32),
            DMA((8,)), DMA((8,)), DMA((n_gx,)), DMA((n_gx,)), DMA((n_yz,)), DMA((n_yz,)),
        ],
        compiler_params=pltpu.CompilerParams(collective_id=1, has_side_effects=True, vmem_limit_bytes=4 * 1024 * 1024),
        name="exchange_max",
    )(send, top)


def first(send_list, pairs, count, own, recv, ends, mobility):
    return pl.pallas_call(
        first_kernel,
        out_shape=(
            shape(3, BLK, LANE), shape(1, LANE), shape(6, BLK, LANE), shape(8, 6 * GB, LANE),
            shape(9, 64, LANE), shape(9, BLK, LANE),
        ),
        in_specs=[SMEM, SMEM, SMEM, VMEM, VMEM, VMEM, VMEM],
        out_specs=(VMEM,) * 6,
        scratch_shapes=[STAGE, BLOCKS] + velocity_scratch(),
        compiler_params=LOCAL,
        name="first",
    )(send_list, pairs, count, own, recv, ends, mobility)


def second(pairs, count, own, ghost, own_v, recv, top, v, ends, mob):
    return pl.pallas_call(
        second_kernel,
        out_shape=shape(3, BLK * LANE),
        in_specs=[SMEM, SMEM] + [VMEM] * 8,
        out_specs=VMEM,
        scratch_shapes=[pltpu.VMEM((9, 64, LANE), F32), STAGE] + velocity_scratch(),
        compiler_params=LOCAL,
        name="second",
    )(pairs, count, own, ghost, own_v, recv, top, v, ends, mob)


def local(nodes, links, burgers, mobility, send_list, pair_list, pair_count):
    own, ends, send = prepare(send_list, nodes, links, burgers)
    recv = exchange(send)
    v, top, own_v, send_v, ghost, mob = first(send_list, pair_list, pair_count, own, recv, ends, mobility)
    recv_v, top_all = exchange_max(send_v, top)
    return second(pair_list, pair_count, own, ghost, own_v, recv_v, top_all, v, ends, mob)


def solution(mesh):
    return jax.shard_map(
        local,
        mesh=mesh,
        in_specs=(
            P(None, ("gx", "yz")),
            P(None, ("gx", "yz")),
            P(None, ("gx", "yz")),
            P(None, None, ("gx", "yz")),
            P(("gx", "yz"), None, None),
            P(None, ("gx", "yz")),
            P(("gx", "yz")),
        ),
        out_specs=P(None, ("gx", "yz")),
        check_vma=False,
    )
```

```python
import functools
import itertools
import math

import jax
import jax.numpy as jnp
from jax import lax
from jax.experimental import pallas as pl
from jax.experimental.pallas import tpu as pltpu
from jax.sharding import PartitionSpec as P

F32 = jnp.float32
BF16 = jnp.bfloat16
A_SQUARED = 0.25
NU_FACTOR = 0.4
DX_LIMIT = 1.0
SPEED_EPS = 1e-05
DIRECTIONS = ((-1, -1), (-1, 0), (-1, 1), (0, -1), (0, 1), (1, -1), (1, 0), (1, 1))
BLK = 32
LANE = 128
GB = 6
SLOTS = BLK + 64
QROWS = 32
FROWS = 48
UNROLL = 16
SCAT = 8
PAIRS = 160
MESH_ID = pl.DeviceIdType.MESH
STAGES = ((("yz", 1, 2),), (("gx", 1, 4), ("yz", 2, 4)), (("gx", 4, 4), ("yz", 8, 4)))


def cross(u, v):
    return [u[1] * v[2] - u[2] * v[1], u[2] * v[0] - u[0] * v[2], u[0] * v[1] - u[1] * v[0]]


def dot3(u, v):
    return u[0] * v[0] + u[1] * v[1] + u[2] * v[2]


def rounded(x):
    return x.astype(BF16).astype(F32)


def split2(x):
    high = rounded(x)
    return high, rounded(x - high)


def split3(x):
    high = rounded(x)
    rest = x - high
    mid = rounded(rest)
    return high, mid, rounded(rest - mid)


def to_rows(src_ref, rows, stage_ref, lead=None):
    for k in range(BLK):
        lanes = pl.ds(k * LANE, LANE)
        piece = src_ref[:, lanes] if lead is None else src_ref[lead, :, lanes]
        stage_ref[8 * k : 8 * k + rows, :] = piece
    return [stage_ref[pl.ds(c, BLK, stride=8), :] for c in range(rows)]


def gather_ends(table_ref, ends):
    outs = []
    for end in ends:
        high = end >> 7
        low = end & 127
        picked = [jnp.zeros((BLK, LANE), F32) for _ in range(3)]
        for row in range(BLK):
            here = high == row
            for c in range(3):
                wide = jnp.broadcast_to(table_ref[c, row : row + 1, :], (BLK, LANE))
                found = jnp.take_along_axis(wide, low, axis=1, mode="promise_in_bounds")
                picked[c] = jnp.where(here, found, picked[c])
        outs.append(picked)
    return outs


def pack_blocks(send_list, block_ref, rows, send_ref):
    for k in range(8):
        for g in range(GB):
            chosen = send_list[g, 0, k]
            send_ref[k, rows * g : rows * (g + 1), :] = block_ref[chosen, 0:rows, :]


def digits(stage):
    place = {"gx": lax.axis_index("gx"), "yz": lax.axis_index("yz")}
    found = []
    for offsets in itertools.product(*[range(size) for _, _, size in stage]):
        if any(offsets):
            peer = dict(place)
            for (axis, stride, size), offset in zip(stage, offsets):
                digit = lax.rem(lax.div(place[axis], stride), size)
                peer[axis] = peer[axis] + (lax.rem(digit + offset, size) - digit) * stride
            found.append((peer["gx"], peer["yz"]))
    return found


def neighbours():
    gx = lax.axis_index("gx")
    yz = lax.axis_index("yz")
    n_gx = lax.axis_size("gx")
    n_yz = lax.axis_size("yz")
    return [(lax.rem(gx + dx + n_gx, n_gx), lax.rem(yz + dy + n_yz, n_yz)) for dx, dy in DIRECTIONS]


def remote(source, target, send_sem, recv_sem, device):
    return pltpu.make_async_remote_copy(
        src_ref=source, dst_ref=target, send_sem=send_sem, recv_sem=recv_sem, device_id=device, device_id_type=MESH_ID
    )


def ghost_copies(send_ref, recv_ref, send_sem, recv_sem, targets):
    return [remote(send_ref.at[k], recv_ref.at[k], send_sem.at[k], recv_sem.at[k], targets[k]) for k in range(8)]


def source_features(mid, line, burg, slot, qs_ref, f_ref):
    def put_q(row, value):
        qs_ref[pl.ds(slot * QROWS + row, BLK, stride=QROWS), :] = value

    def put_f(row, value):
        f_ref[pl.ds(slot * FROWS + row, BLK, stride=FROWS), :] = value

    row = 0
    for c in range(3):
        high, middle, low = split3(mid[c])
        for part in (high, high, middle, middle, high, low):
            put_q(row, part)
            row += 1
    for part in split3(dot3(mid, mid) + A_SQUARED):
        put_q(row, part)
        row += 1
    one = jnp.ones((BLK, LANE), F32)
    zero = jnp.zeros((BLK, LANE), F32)
    for _ in range(3):
        put_q(row, one)
        row += 1
    while row < QROWS:
        put_q(row, zero)
        row += 1
    moment = cross(burg, mid)
    for a in range(3):
        for d in range(3):
            high, low = split2(line[a] * burg[d])
            put_f(3 * a + d, high)
            put_f(24 + 3 * a + d, low)
            high, low = split2(line[a] * moment[d])
            put_f(9 + 3 * a + d, high)
            put_f(33 + 3 * a + d, low)


def target_features(mid, qt_ref):
    def put(row, value):
        qt_ref[pl.ds(row, BLK, stride=QROWS), :] = value

    row = 0
    for c in range(3):
        high, middle, low = split3(-2.0 * mid[c])
        for part in (high, middle, high, middle, low, high):
            put(row, part)
            row += 1
    one = jnp.ones((BLK, LANE), F32)
    zero = jnp.zeros((BLK, LANE), F32)
    for _ in range(3):
        put(row, one)
        row += 1
    for part in split3(dot3(mid, mid)):
        put(row, part)
        row += 1
    while row < QROWS:
        put(row, zero)
        row += 1


def velocity(own, fill_ghost, ghost, pairs, pair_row, count, ends_ref, mob_ref, scr):
    qs_f, qt_f, f_f, qs_b, qt_b, f_b, acc, force_ref = scr
    centre = [jnp.mean(own[c]) for c in range(3)]
    mid = [own[c] - centre[c] for c in range(3)]
    line = own[3:6]
    burg = own[6:9]
    source_features(mid, line, burg, 0, qs_f, f_f)
    target_features(mid, qt_f)
    fill_ghost()
    for half in range(2):
        rows = [ghost(c, half) for c in range(9)]
        source_features([rows[c] - centre[c] for c in range(3)], rows[3:6], rows[6:9], BLK * (half + 1), qs_f, f_f)

    def convert(step, carry):
        for j in range(4):
            slot = 4 * step + j
            q = qs_f[pl.ds(pl.multiple_of(slot * QROWS, 8), QROWS), :]
            qs_b[slot] = jnp.transpose(q).astype(BF16)
            f = f_f[pl.ds(pl.multiple_of(slot * FROWS, 8), FROWS), :].astype(BF16)
            f_b[slot] = jnp.concatenate([f, f], axis=1)
        return carry

    lax.fori_loop(0, SLOTS // 4, convert, 0)

    def convert_target(step, carry):
        for j in range(4):
            slot = 4 * step + j
            qt_b[slot] = qt_f[pl.ds(pl.multiple_of(slot * QROWS, 8), QROWS), :].astype(BF16)
        return carry

    lax.fori_loop(0, BLK // 4, convert_target, 0)
    def pair_step(step, carry):
        for j in range(UNROLL):
            place = UNROLL * step + j
            target = jnp.minimum(pairs[0, place], BLK - 1)
            source = pairs[1, place]
            ghost_place = source - BLK
            group = (ghost_place * 43) >> 8
            slot = jnp.where(source < BLK, source, BLK + 8 * group + (ghost_place - GB * group))
            dist = jnp.dot(qs_b[slot], qt_b[target], preferred_element_type=F32)
            root = lax.rsqrt(dist)
            weight = root * root * root
            high = weight.astype(BF16)
            low = (weight - high.astype(F32)).astype(BF16)
            both = jnp.concatenate([high, low], axis=0)
            found = jnp.dot(f_b[slot], both, preferred_element_type=F32)
            acc[:, place, :] = found[0:24] + found[24:48]
        return carry

    lax.fori_loop(0, PAIRS // UNROLL, pair_step, 0)
    pair_id = lax.broadcasted_iota(jnp.int32, (BLK, PAIRS), 1)
    block_id = lax.broadcasted_iota(jnp.int32, (BLK, PAIRS), 0)
    chosen = jnp.where((block_id == pair_row[0:1, :]) & (pair_id < count), 1.0, 0.0).astype(BF16)
    chosen = jnp.concatenate([chosen, chosen], axis=1)

    def total(row):
        high = acc[row].astype(BF16)
        low = (acc[row] - high.astype(F32)).astype(BF16)
        return jnp.dot(chosen, jnp.concatenate([high, low], axis=0), preferred_element_type=F32)

    s_mat = [[total(3 * a + d) for d in range(3)] for a in range(3)]
    t_mat = [[total(9 + 3 * a + d) for d in range(3)] for a in range(3)]
    arm = cross(mid, burg)
    lined_s = [burg[0] * s_mat[0][d] + burg[1] * s_mat[1][d] + burg[2] * s_mat[2][d] for d in range(3)]
    lined_t = [burg[0] * t_mat[0][d] + burg[1] * t_mat[1][d] + burg[2] * t_mat[2][d] for d in range(3)]
    swept = cross(lined_s, mid)
    skew = [s_mat[2][1] - s_mat[1][2], s_mat[0][2] - s_mat[2][0], s_mat[1][0] - s_mat[0][1]]
    twist = NU_FACTOR * (dot3(mid, skew) + (t_mat[0][0] + t_mat[1][1] + t_mat[2][2]))
    traction = [
        0.5 * ((dot3(s_mat[k], arm) - dot3(t_mat[k], burg)) + (swept[k] - lined_t[k])) + twist * burg[k]
        for k in range(3)
    ]
    force = cross(traction, line)
    for c in range(3):
        high, low = split2(0.5 * force[c])
        force_ref[2 * c] = high
        force_ref[2 * c + 1] = low

    row_id = lax.broadcasted_iota(jnp.int32, (BLK, LANE), 0)
    lane_id = lax.broadcasted_iota(jnp.int32, (LANE, LANE), 0)

    def scatter_step(step, nodal):
        lhs = []
        rhs = []
        for j in range(SCAT):
            k = SCAT * step + j
            for e in range(2):
                end = ends_ref[e, pl.ds(k, 1), :]
                here = row_id == (end >> 7)
                lhs.append(
                    jnp.concatenate(
                        [jnp.where(here, force_ref[i, pl.ds(k, 1), :], 0.0).astype(BF16) for i in range(6)], axis=0
                    )
                )
                rhs.append(jnp.where(lane_id == (end & 127), 1.0, 0.0).astype(BF16))
        return nodal + lax.dot_general(
            jnp.concatenate(lhs, axis=1),
            jnp.concatenate(rhs, axis=1),
            (((1,), (1,)), ((), ())),
            preferred_element_type=F32,
        )

    nodal = lax.fori_loop(0, BLK // SCAT, scatter_step, jnp.zeros((6 * BLK, LANE), F32))
    pulled = [nodal[2 * BLK * c : 2 * BLK * c + BLK] + nodal[2 * BLK * c + BLK : 2 * BLK * (c + 1)] for c in range(3)]
    return [dot3([mob_ref[3 * r + c] for c in range(3)], pulled) for r in range(3)]


def step_kernel(
    stages, send_list, pairs, count_ref, pair_row, nodes_hbm, links_hbm, burgers_hbm, mobility_hbm, out_ref,
    nodes_ref, links_ref, burgers_ref, mobility_ref, in_sem,
    own_ref, own_v_ref, v_ref, ends_ref, mob_ref, ghost_ref, stage_ref, block_ref,
    send_ref, recv_ref, send_v_ref, recv_v_ref, box_ref, mid_ref, gs1, gr1, gs2, gr2, ms, mr, *scr
):
    loads = [
        pltpu.make_async_copy(src, dst, in_sem.at[i])
        for i, (src, dst) in enumerate(
            ((nodes_hbm, nodes_ref), (links_hbm, links_ref), (burgers_hbm, burgers_ref), (mobility_hbm, mobility_ref))
        )
    ]
    for load in loads:
        load.start()
    targets = neighbours()
    lines = [digits(stage) for stage in stages]
    peers = targets + [peer for line in lines for peer in line]
    barrier = pltpu.get_barrier_semaphore()
    for peer in peers:
        pl.semaphore_signal(barrier, inc=1, device_id=peer, device_id_type=MESH_ID)
    count = count_ref[0]

    loads[0].wait()
    coords = to_rows(nodes_ref, 3, stage_ref)
    for c in range(3):
        v_ref[c] = coords[c]
    loads[1].wait()
    for k in range(BLK):
        lanes = pl.ds(k * LANE, LANE)
        ends_ref[0, k : k + 1, :] = links_ref[0:1, lanes]
        ends_ref[1, k : k + 1, :] = links_ref[1:2, lanes]
    first, second = gather_ends(v_ref, [ends_ref[0], ends_ref[1]])
    loads[2].wait()
    rows = [0.5 * (first[c] + second[c]) for c in range(3)] + [second[c] - first[c] for c in range(3)]
    rows = rows + to_rows(burgers_ref, 3, stage_ref)
    for c in range(9):
        own_ref[c] = rows[c]
        for k in range(BLK):
            block_ref[k, c : c + 1, :] = rows[c][k : k + 1]
    pack_blocks(send_list, block_ref, 9, send_ref)
    pl.semaphore_wait(barrier, len(peers))
    copies = ghost_copies(send_ref, recv_ref, gs1, gr1, targets)
    for copy in copies:
        copy.start()
    loads[3].wait()
    for r in range(3):
        rows = to_rows(mobility_ref, 3, stage_ref, r)
        for c in range(3):
            mob_ref[3 * r + c] = rows[c]

    def fill_first():
        for copy in copies:
            copy.wait_recv()
        for c in range(9):
            for k in range(8):
                ghost_ref[c, 8 * k : 8 * k + GB, :] = recv_ref[k, pl.ds(c, GB, stride=9), :]
                ghost_ref[c, 8 * k + GB : 8 * k + 8, :] = jnp.zeros((8 - GB, LANE), F32)

    def ghost(c, half):
        return ghost_ref[c, BLK * half : BLK * (half + 1), :]

    own = [own_ref[c] for c in range(9)]
    speed = velocity(own, fill_first, ghost, pairs, pair_row, count, ends_ref, mob_ref, scr)
    best = jnp.max(dot3(speed, speed), axis=0, keepdims=True)
    waiting = []

    def spread(stage, value):
        base = sum(len(line) for line in lines[:stage])
        mid_ref[stage] = value
        sent = [
            remote(mid_ref.at[stage], box_ref.at[base + o], ms.at[base + o], mr.at[base + o], peer)
            for o, peer in enumerate(lines[stage])
        ]
        for copy in sent:
            copy.start()
        waiting.extend(sent)
        return base, sent

    def settle(state, value):
        base, sent = state
        for copy in sent:
            copy.wait_recv()
        for o in range(len(sent)):
            value = jnp.maximum(value, box_ref[base + o])
        return value

    state = spread(0, best)
    for c in range(3):
        v_ref[c] = speed[c]
    best = settle(state, best)
    state = spread(1, best)
    first, second = gather_ends(v_ref, [ends_ref[0], ends_ref[1]])
    rows = [0.5 * (first[c] + second[c]) for c in range(3)] + [second[c] - first[c] for c in range(3)]
    for c in range(6):
        own_v_ref[c] = rows[c]
        for k in range(BLK):
            block_ref[k, c : c + 1, :] = rows[c][k : k + 1]
    pack_blocks(send_list, block_ref, 6, send_v_ref)
    copies_v = ghost_copies(send_v_ref, recv_v_ref, gs2, gr2, targets)
    for copy in copies_v:
        copy.start()
    best = settle(state, best)
    state = spread(2, best)
    best = settle(state, best)
    step = DX_LIMIT / (jnp.sqrt(jnp.max(best)) + SPEED_EPS)

    def fill_second():
        for copy in copies_v:
            copy.wait_recv()
        for c in range(6):
            for k in range(8):
                rows = slice(8 * k, 8 * k + GB)
                ghost_ref[c, rows, :] = ghost_ref[c, rows, :] + step * recv_v_ref[k, pl.ds(c, GB, stride=6), :]

    own = [own_ref[c] + step * own_v_ref[c] if c < 6 else own_ref[c] for c in range(9)]
    speed = velocity(own, fill_second, ghost, pairs, pair_row, count, ends_ref, mob_ref, scr)
    for c in range(3):
        stage_ref[pl.ds(c, BLK, stride=8), :] = 0.5 * step * (v_ref[c] + speed[c])
    for k in range(BLK):
        out_ref[:, pl.ds(k * LANE, LANE)] = stage_ref[8 * k : 8 * k + 3, :]
    for copy in copies + copies_v + waiting:
        copy.wait_send()


VMEM = pl.BlockSpec(memory_space=pltpu.VMEM)
SMEM = pl.BlockSpec(memory_space=pltpu.SMEM)
ANY = pl.BlockSpec(memory_space=pl.ANY)
DMA = pltpu.SemaphoreType.DMA


def local(nodes, links, burgers, mobility, send_list, pair_list, pair_count):
    n_gx = lax.axis_size("gx")
    n_yz = lax.axis_size("yz")
    stages = STAGES
    mail = sum(math.prod(size for _, _, size in stage) - 1 for stage in stages)
    scratch = [
        pltpu.VMEM((3, BLK * LANE), F32),
        pltpu.VMEM((2, BLK * LANE), jnp.int32),
        pltpu.VMEM((3, BLK * LANE), F32),
        pltpu.VMEM((3, 3, BLK * LANE), F32),
        DMA((4,)),
        pltpu.VMEM((9, BLK, LANE), F32),
        pltpu.VMEM((6, BLK, LANE), F32),
        pltpu.VMEM((3, BLK, LANE), F32),
        pltpu.VMEM((2, BLK, LANE), jnp.int32),
        pltpu.VMEM((9, BLK, LANE), F32),
        pltpu.VMEM((9, 64, LANE), F32),
        pltpu.VMEM((BLK * 8, LANE), F32),
        pltpu.VMEM((BLK, 16, LANE), F32),
        pltpu.VMEM((8, 9 * GB, LANE), F32),
        pltpu.VMEM((8, 9 * GB, LANE), F32),
        pltpu.VMEM((8, 6 * GB, LANE), F32),
        pltpu.VMEM((8, 6 * GB, LANE), F32),
        pltpu.VMEM((mail, 1, LANE), F32),
        pltpu.VMEM((len(stages), 1, LANE), F32),
        DMA((8,)), DMA((8,)), DMA((8,)), DMA((8,)), DMA((mail,)), DMA((mail,)),
        pltpu.VMEM((SLOTS * QROWS, LANE), F32),
        pltpu.VMEM((BLK * QROWS, LANE), F32),
        pltpu.VMEM((SLOTS * FROWS, LANE), F32),
        pltpu.VMEM((SLOTS, LANE, QROWS), BF16),
        pltpu.VMEM((BLK, QROWS, LANE), BF16),
        pltpu.VMEM((SLOTS, FROWS, 2 * LANE), BF16),
        pltpu.VMEM((24, PAIRS, LANE), F32),
        pltpu.VMEM((6, BLK, LANE), F32),
    ]
    return pl.pallas_call(
        functools.partial(step_kernel, stages),
        out_shape=jax.ShapeDtypeStruct((3, BLK * LANE), F32),
        in_specs=[SMEM, SMEM, SMEM, VMEM, ANY, ANY, ANY, ANY],
        out_specs=VMEM,
        scratch_shapes=scratch,
        compiler_params=pltpu.CompilerParams(collective_id=0, has_side_effects=True, vmem_limit_bytes=56 * 1024 * 1024),
        name="step",
    )(jnp.transpose(send_list, (2, 0, 1)), pair_list, pair_count, pair_list, nodes, links, burgers, mobility)


def solution(mesh):
    return jax.shard_map(
        local,
        mesh=mesh,
        in_specs=(
            P(None, ("gx", "yz")),
            P(None, ("gx", "yz")),
            P(None, ("gx", "yz")),
            P(None, None, ("gx", "yz")),
            P(("gx", "yz"), None, None),
            P(None, ("gx", "yz")),
            P(("gx", "yz")),
        ),
        out_specs=P(None, ("gx", "yz")),
        check_vma=False,
    )
```

```python
import functools
import itertools
import math

import jax
import jax.numpy as jnp
from jax import lax
from jax.experimental import pallas as pl
from jax.experimental.pallas import tpu as pltpu
from jax.sharding import PartitionSpec as P

F32 = jnp.float32
BF16 = jnp.bfloat16
A_SQUARED = 0.25
NU_FACTOR = 0.4
DX_LIMIT = 1.0
SPEED_EPS = 1e-05
DIRECTIONS = ((-1, -1), (-1, 0), (-1, 1), (0, -1), (0, 1), (1, -1), (1, 0), (1, 1))
BLK = 32
LANE = 128
GB = 6
SLOTS = BLK + 64
QRAW = 8
FRAW = 24
CONV = 8
QK = 6 * QRAW
UNROLL = 32
SCAT = 16
PAIRS = 160
MESH_ID = pl.DeviceIdType.MESH
STAGES = ((("yz", 1, 2),), (("gx", 1, 4), ("yz", 2, 4)), (("gx", 4, 4), ("yz", 8, 4)))


def cross(u, v):
    return [u[1] * v[2] - u[2] * v[1], u[2] * v[0] - u[0] * v[2], u[0] * v[1] - u[1] * v[0]]


def dot3(u, v):
    return u[0] * v[0] + u[1] * v[1] + u[2] * v[2]


def rounded(x):
    return x.astype(BF16).astype(F32)


def split2(x):
    high = rounded(x)
    return high, rounded(x - high)


def split3(x):
    high = rounded(x)
    rest = x - high
    mid = rounded(rest)
    return high, mid, rounded(rest - mid)


def to_rows(src_ref, rows, stage_ref, lead=None):
    for k in range(BLK):
        lanes = pl.ds(k * LANE, LANE)
        piece = src_ref[:, lanes] if lead is None else src_ref[lead, :, lanes]
        stage_ref[8 * k : 8 * k + rows, :] = piece
    return [stage_ref[pl.ds(c, BLK, stride=8), :] for c in range(rows)]


def gather_ends(table_ref, ends):
    outs = []
    for end in ends:
        high = end >> 7
        low = end & 127
        picked = [jnp.zeros((BLK, LANE), F32) for _ in range(3)]
        for row in range(BLK):
            here = high == row
            for c in range(3):
                wide = jnp.broadcast_to(table_ref[c, row : row + 1, :], (BLK, LANE))
                found = jnp.take_along_axis(wide, low, axis=1, mode="promise_in_bounds")
                picked[c] = jnp.where(here, found, picked[c])
        outs.append(picked)
    return outs


def pack_blocks(send_list, block_ref, rows, send_ref):
    for k in range(8):
        for g in range(GB):
            chosen = send_list[g, 0, k]
            send_ref[k, rows * g : rows * (g + 1), :] = block_ref[chosen, 0:rows, :]


def digits(stage):
    place = {"gx": lax.axis_index("gx"), "yz": lax.axis_index("yz")}
    found = []
    for offsets in itertools.product(*[range(size) for _, _, size in stage]):
        if any(offsets):
            peer = dict(place)
            for (axis, stride, size), offset in zip(stage, offsets):
                digit = lax.rem(lax.div(place[axis], stride), size)
                peer[axis] = peer[axis] + (lax.rem(digit + offset, size) - digit) * stride
            found.append((peer["gx"], peer["yz"]))
    return found


def neighbours():
    gx = lax.axis_index("gx")
    yz = lax.axis_index("yz")
    n_gx = lax.axis_size("gx")
    n_yz = lax.axis_size("yz")
    return [(lax.rem(gx + dx + n_gx, n_gx), lax.rem(yz + dy + n_yz, n_yz)) for dx, dy in DIRECTIONS]


def remote(source, target, send_sem, recv_sem, device):
    return pltpu.make_async_remote_copy(
        src_ref=source, dst_ref=target, send_sem=send_sem, recv_sem=recv_sem, device_id=device, device_id_type=MESH_ID
    )


def ghost_copies(send_ref, recv_ref, send_sem, recv_sem, targets):
    return [remote(send_ref.at[k], recv_ref.at[k], send_sem.at[k], recv_sem.at[k], targets[k]) for k in range(8)]


def put_rows(ref, slot, height, values):
    for row, value in enumerate(values):
        if value is not None:
            ref[pl.ds(slot * height + row, BLK, stride=height), :] = value


def filled(value):
    return jnp.full((BLK, LANE), value, F32)


def spread_features(order, slot, mid, line, burg, slope, q_refs, f_refs):
    moment = cross(burg, mid)
    if order == 0:
        put_rows(q_refs[0], slot, QRAW, mid + [dot3(mid, mid) + A_SQUARED, filled(1.0)] + [filled(0.0)] * 3)
        put_rows(f_refs[0], slot, FRAW, [line[a] * burg[d] for a in range(3) for d in range(3)])
        put_rows(f_refs[0], slot, FRAW, [None] * 9 + [line[a] * moment[d] for a in range(3) for d in range(3)])
        return
    mid_v, line_v = slope
    moment_v = cross(burg, mid_v)
    put_rows(q_refs[1], slot, QRAW, mid_v + [2.0 * dot3(mid, mid_v), dot3(mid_v, mid_v)] + [filled(0.0)] * 3)
    put_rows(f_refs[1], slot, FRAW, [line_v[a] * burg[d] for a in range(3) for d in range(3)])
    put_rows(
        f_refs[1], slot, FRAW,
        [None] * 9 + [line[a] * moment_v[d] + line_v[a] * moment[d] for a in range(3) for d in range(3)],
    )
    put_rows(f_refs[2], slot, FRAW, [filled(0.0)] * 9 + [line_v[a] * moment_v[d] for a in range(3) for d in range(3)])


def over_slots(own, ghosts, body):
    def own_trip(trip, carry):
        for j in range(CONV):
            body(CONV * trip + j)
        return carry

    def ghost_trip(trip, carry):
        for j in range(GB):
            body(BLK + 8 * trip + j)
        return carry

    if own:
        lax.fori_loop(0, BLK // CONV, own_trip, 0)
    if ghosts:
        lax.fori_loop(0, 8, ghost_trip, 0)


def turn_sources(order, own, ghosts, q_refs, qs_b):
    def body(slot):
        rows = pl.ds(pl.multiple_of(slot * QRAW, 8), QRAW)
        high, mid, low = split3(q_refs[order][rows, :])
        turned = jnp.transpose(jnp.concatenate([high, high, mid, mid, high, low], axis=0)).astype(BF16)
        qs_b[slot, :, QK * order : QK * (order + 1)] = turned

    over_slots(own, ghosts, body)


def convert_features(own, ghosts, step, f_refs, f_b):
    def body(slot):
        rows = pl.ds(pl.multiple_of(slot * FRAW, 8), FRAW)
        value = f_refs[0][rows, :]
        if step is not None:
            value = value + step * (f_refs[1][rows, :] + step * f_refs[2][rows, :])
        high, low = split2(value)
        part = jnp.concatenate([high, low], axis=0).astype(BF16)
        f_b[slot, :, 0:LANE] = part
        f_b[slot, :, LANE : 2 * LANE] = part

    over_slots(own, ghosts, body)


def convert_targets(mid, step, t_refs, qt_b):
    put_rows(t_refs[0], 0, QRAW, [-2.0 * mid[c] for c in range(3)] + [filled(1.0), dot3(mid, mid)] + [filled(0.0)] * 3)
    orders = 1
    if step is not None:
        orders = 2
        flat = filled(1.0) * step
        put_rows(t_refs[1], 0, QRAW, [-2.0 * step * mid[c] for c in range(3)] + [flat, step * flat] + [filled(0.0)] * 3)

    def body(trip, carry):
        for j in range(CONV):
            slot = CONV * trip + j
            for order in range(orders):
                high, mid_part, low = split3(t_refs[order][pl.ds(pl.multiple_of(slot * QRAW, 8), QRAW), :])
                qt_b[slot, QK * order : QK * (order + 1), :] = jnp.concatenate(
                    [high, mid_part, high, mid_part, low, high], axis=0
                ).astype(BF16)
        return carry

    lax.fori_loop(0, BLK // CONV, body, 0)


def pair_sums(depth, mid, line, burg, pairs, pair_row, count, ends_ref, mob_ref, qs_b, qt_b, f_b, acc, force_ref):
    def pair_step(step, carry):
        for j in range(UNROLL):
            place = UNROLL * step + j
            target = jnp.minimum(pairs[0, place], BLK - 1)
            source = pairs[1, place]
            ghost_place = source - BLK
            group = (ghost_place * 43) >> 8
            slot = jnp.where(source < BLK, source, BLK + 8 * group + (ghost_place - GB * group))
            dist = jnp.dot(qs_b[slot, :, 0:depth], qt_b[target, 0:depth, :], preferred_element_type=F32)
            root = lax.rsqrt(dist)
            weight = root * root * root
            high = weight.astype(BF16)
            low = (weight - high.astype(F32)).astype(BF16)
            both = jnp.concatenate([high, low], axis=0)
            found = jnp.dot(f_b[slot], both, preferred_element_type=F32)
            acc[:, place, :] = found[0:FRAW] + found[FRAW : 2 * FRAW]
        return carry

    lax.fori_loop(0, PAIRS // UNROLL, pair_step, 0)
    pair_id = lax.broadcasted_iota(jnp.int32, (BLK, PAIRS), 1)
    block_id = lax.broadcasted_iota(jnp.int32, (BLK, PAIRS), 0)
    chosen = jnp.where((block_id == pair_row[0:1, :]) & (pair_id < count), 1.0, 0.0).astype(BF16)
    chosen = jnp.concatenate([chosen, chosen], axis=1)

    def total(row):
        high = acc[row].astype(BF16)
        low = (acc[row] - high.astype(F32)).astype(BF16)
        return jnp.dot(chosen, jnp.concatenate([high, low], axis=0), preferred_element_type=F32)

    s_mat = [[total(3 * a + d) for d in range(3)] for a in range(3)]
    t_mat = [[total(9 + 3 * a + d) for d in range(3)] for a in range(3)]
    arm = cross(mid, burg)
    lined_s = [burg[0] * s_mat[0][d] + burg[1] * s_mat[1][d] + burg[2] * s_mat[2][d] for d in range(3)]
    lined_t = [burg[0] * t_mat[0][d] + burg[1] * t_mat[1][d] + burg[2] * t_mat[2][d] for d in range(3)]
    swept = cross(lined_s, mid)
    skew = [s_mat[2][1] - s_mat[1][2], s_mat[0][2] - s_mat[2][0], s_mat[1][0] - s_mat[0][1]]
    twist = NU_FACTOR * (dot3(mid, skew) + (t_mat[0][0] + t_mat[1][1] + t_mat[2][2]))
    traction = [
        0.5 * ((dot3(s_mat[k], arm) - dot3(t_mat[k], burg)) + (swept[k] - lined_t[k])) + twist * burg[k]
        for k in range(3)
    ]
    force = cross(traction, line)
    for c in range(3):
        high, low = split2(0.5 * force[c])
        force_ref[2 * c] = high
        force_ref[2 * c + 1] = low

    row_id = lax.broadcasted_iota(jnp.int32, (BLK, LANE), 0)
    lane_id = lax.broadcasted_iota(jnp.int32, (LANE, LANE), 0)

    def scatter_step(step, nodal):
        lhs = []
        rhs = []
        for j in range(SCAT):
            k = SCAT * step + j
            for e in range(2):
                end = ends_ref[e, pl.ds(k, 1), :]
                here = row_id == (end >> 7)
                lhs.append(
                    jnp.concatenate(
                        [jnp.where(here, force_ref[i, pl.ds(k, 1), :], 0.0).astype(BF16) for i in range(6)], axis=0
                    )
                )
                rhs.append(jnp.where(lane_id == (end & 127), 1.0, 0.0).astype(BF16))
        return nodal + lax.dot_general(
            jnp.concatenate(lhs, axis=1),
            jnp.concatenate(rhs, axis=1),
            (((1,), (1,)), ((), ())),
            preferred_element_type=F32,
        )

    nodal = lax.fori_loop(0, BLK // SCAT, scatter_step, jnp.zeros((6 * BLK, LANE), F32))
    pulled = [nodal[2 * BLK * c : 2 * BLK * c + BLK] + nodal[2 * BLK * c + BLK : 2 * BLK * (c + 1)] for c in range(3)]
    return [dot3([mob_ref[3 * r + c] for c in range(3)], pulled) for r in range(3)]


def step_kernel(
    stages, send_list, pairs, count_ref, pair_row, nodes_hbm, links_hbm, burgers_hbm, mobility_hbm, out_ref,
    nodes_ref, links_ref, burgers_ref, mobility_ref, in_sem,
    own_ref, own_v_ref, v_ref, ends_ref, mob_ref, ghost_ref, ghost_v_ref, stage_ref, block_ref,
    send_ref, recv_ref, send_v_ref, recv_v_ref, box_ref, mid_ref, gs1, gr1, gs2, gr2, ms, mr,
    q0_ref, q1_ref, f0_ref, f1_ref, f2_ref, t0_ref, t1_ref, qs_b, qt_b, f_b, acc, force_ref
):
    loads = [
        pltpu.make_async_copy(src, dst, in_sem.at[i])
        for i, (src, dst) in enumerate(
            ((nodes_hbm, nodes_ref), (links_hbm, links_ref), (burgers_hbm, burgers_ref), (mobility_hbm, mobility_ref))
        )
    ]
    for load in loads:
        load.start()
    targets = neighbours()
    lines = [digits(stage) for stage in stages]
    peers = targets + [peer for line in lines for peer in line]
    barrier = pltpu.get_barrier_semaphore()
    for peer in peers:
        pl.semaphore_signal(barrier, inc=1, device_id=peer, device_id_type=MESH_ID)
    count = count_ref[0]

    loads[0].wait()
    coords = to_rows(nodes_ref, 3, stage_ref)
    for c in range(3):
        v_ref[c] = coords[c]
    loads[1].wait()
    for k in range(BLK):
        lanes = pl.ds(k * LANE, LANE)
        ends_ref[0, k : k + 1, :] = links_ref[0:1, lanes]
        ends_ref[1, k : k + 1, :] = links_ref[1:2, lanes]
    first, second = gather_ends(v_ref, [ends_ref[0], ends_ref[1]])
    loads[2].wait()
    rows = [0.5 * (first[c] + second[c]) for c in range(3)] + [second[c] - first[c] for c in range(3)]
    rows = rows + to_rows(burgers_ref, 3, stage_ref)
    for c in range(9):
        own_ref[c] = rows[c]
        for k in range(BLK):
            block_ref[k, c : c + 1, :] = rows[c][k : k + 1]
    pack_blocks(send_list, block_ref, 9, send_ref)
    pl.semaphore_wait(barrier, len(peers))
    copies = ghost_copies(send_ref, recv_ref, gs1, gr1, targets)
    for copy in copies:
        copy.start()
    loads[3].wait()
    for r in range(3):
        rows = to_rows(mobility_ref, 3, stage_ref, r)
        for c in range(3):
            mob_ref[3 * r + c] = rows[c]

    q_refs = (q0_ref, q1_ref)
    t_refs = (t0_ref, t1_ref)
    f_refs = (f0_ref, f1_ref, f2_ref)
    tables = (qs_b, qt_b, f_b, acc, force_ref)
    own = [own_ref[c] for c in range(9)]
    centre = [jnp.mean(own[c]) for c in range(3)]
    mid = [own[c] - centre[c] for c in range(3)]
    spread_features(0, 0, mid, own[3:6], own[6:9], None, q_refs, f_refs)
    turn_sources(0, True, False, q_refs, qs_b)
    convert_features(True, False, None, f_refs, f_b)
    convert_targets(mid, None, t_refs, qt_b)
    for copy in copies:
        copy.wait_recv()
    for c in range(9):
        for k in range(8):
            ghost_ref[c, 8 * k : 8 * k + GB, :] = recv_ref[k, pl.ds(c, GB, stride=9), :]
            ghost_ref[c, 8 * k + GB : 8 * k + 8, :] = jnp.zeros((8 - GB, LANE), F32)
            if c < 6:
                ghost_v_ref[c, 8 * k + GB : 8 * k + 8, :] = jnp.zeros((8 - GB, LANE), F32)

    def ghost(half):
        rows = [ghost_ref[c, BLK * half : BLK * (half + 1), :] for c in range(9)]
        return [rows[c] - centre[c] for c in range(3)], rows[3:6], rows[6:9]

    for half in range(2):
        spread_features(0, BLK * (half + 1), *ghost(half), None, q_refs, f_refs)
    turn_sources(0, False, True, q_refs, qs_b)
    convert_features(False, True, None, f_refs, f_b)
    speed = pair_sums(QK, mid, own[3:6], own[6:9], pairs, pair_row, count, ends_ref, mob_ref, *tables)
    best = jnp.max(dot3(speed, speed), axis=0, keepdims=True)
    waiting = []

    def spread(stage, value):
        base = sum(len(line) for line in lines[:stage])
        mid_ref[stage] = value
        sent = [
            remote(mid_ref.at[stage], box_ref.at[base + o], ms.at[base + o], mr.at[base + o], peer)
            for o, peer in enumerate(lines[stage])
        ]
        for copy in sent:
            copy.start()
        waiting.extend(sent)
        return base, sent

    def settle(state, value):
        base, sent = state
        for copy in sent:
            copy.wait_recv()
        for o in range(len(sent)):
            value = jnp.maximum(value, box_ref[base + o])
        return value

    state = spread(0, best)
    for c in range(3):
        v_ref[c] = speed[c]
    best = settle(state, best)
    state = spread(1, best)
    first, second = gather_ends(v_ref, [ends_ref[0], ends_ref[1]])
    rows = [0.5 * (first[c] + second[c]) for c in range(3)] + [second[c] - first[c] for c in range(3)]
    for c in range(6):
        own_v_ref[c] = rows[c]
        for k in range(BLK):
            block_ref[k, c : c + 1, :] = rows[c][k : k + 1]
    pack_blocks(send_list, block_ref, 6, send_v_ref)
    copies_v = ghost_copies(send_v_ref, recv_v_ref, gs2, gr2, targets)
    for copy in copies_v:
        copy.start()
    best = settle(state, best)
    state = spread(2, best)
    own = [own_ref[c] for c in range(9)]
    mid = [own[c] - centre[c] for c in range(3)]
    own_v = [own_v_ref[c] for c in range(6)]
    spread_features(1, 0, mid, own[3:6], own[6:9], (own_v[0:3], own_v[3:6]), q_refs, f_refs)
    turn_sources(1, True, False, q_refs, qs_b)
    for copy in copies_v:
        copy.wait_recv()
    for c in range(6):
        for k in range(8):
            ghost_v_ref[c, 8 * k : 8 * k + GB, :] = recv_v_ref[k, pl.ds(c, GB, stride=6), :]
    for half in range(2):
        moving = [ghost_v_ref[c, BLK * half : BLK * (half + 1), :] for c in range(6)]
        spread_features(1, BLK * (half + 1), *ghost(half), (moving[0:3], moving[3:6]), q_refs, f_refs)
    turn_sources(1, False, True, q_refs, qs_b)
    best = settle(state, best)
    step = DX_LIMIT / (jnp.sqrt(jnp.max(best)) + SPEED_EPS)
    convert_features(True, True, step, f_refs, f_b)
    mid = [mid[c] + step * own_v[c] for c in range(3)]
    line = [own[3 + c] + step * own_v[3 + c] for c in range(3)]
    convert_targets(mid, step, t_refs, qt_b)
    speed = pair_sums(2 * QK, mid, line, own[6:9], pairs, pair_row, count, ends_ref, mob_ref, *tables)
    for c in range(3):
        stage_ref[pl.ds(c, BLK, stride=8), :] = 0.5 * step * (v_ref[c] + speed[c])
    for k in range(BLK):
        out_ref[:, pl.ds(k * LANE, LANE)] = stage_ref[8 * k : 8 * k + 3, :]
    for copy in copies + copies_v + waiting:
        copy.wait_send()


VMEM = pl.BlockSpec(memory_space=pltpu.VMEM)
SMEM = pl.BlockSpec(memory_space=pltpu.SMEM)
ANY = pl.BlockSpec(memory_space=pl.ANY)
DMA = pltpu.SemaphoreType.DMA


def local(nodes, links, burgers, mobility, send_list, pair_list, pair_count):
    n_gx = lax.axis_size("gx")
    n_yz = lax.axis_size("yz")
    stages = STAGES
    mail = sum(math.prod(size for _, _, size in stage) - 1 for stage in stages)
    scratch = [
        pltpu.VMEM((3, BLK * LANE), F32),
        pltpu.VMEM((2, BLK * LANE), jnp.int32),
        pltpu.VMEM((3, BLK * LANE), F32),
        pltpu.VMEM((3, 3, BLK * LANE), F32),
        DMA((4,)),
        pltpu.VMEM((9, BLK, LANE), F32),
        pltpu.VMEM((6, BLK, LANE), F32),
        pltpu.VMEM((3, BLK, LANE), F32),
        pltpu.VMEM((2, BLK, LANE), jnp.int32),
        pltpu.VMEM((9, BLK, LANE), F32),
        pltpu.VMEM((9, 64, LANE), F32),
        pltpu.VMEM((6, 64, LANE), F32),
        pltpu.VMEM((BLK * 8, LANE), F32),
        pltpu.VMEM((BLK, 16, LANE), F32),
        pltpu.VMEM((8, 9 * GB, LANE), F32),
        pltpu.VMEM((8, 9 * GB, LANE), F32),
        pltpu.VMEM((8, 6 * GB, LANE), F32),
        pltpu.VMEM((8, 6 * GB, LANE), F32),
        pltpu.VMEM((mail, 1, LANE), F32),
        pltpu.VMEM((len(stages), 1, LANE), F32),
        DMA((8,)), DMA((8,)), DMA((8,)), DMA((8,)), DMA((mail,)), DMA((mail,)),
        *[pltpu.VMEM((SLOTS * QRAW, LANE), F32)] * 2,
        *[pltpu.VMEM((SLOTS * FRAW, LANE), F32)] * 3,
        *[pltpu.VMEM((BLK * QRAW, LANE), F32)] * 2,
        pltpu.VMEM((SLOTS, LANE, 2 * QK), BF16),
        pltpu.VMEM((BLK, 2 * QK, LANE), BF16),
        pltpu.VMEM((SLOTS, 2 * FRAW, 2 * LANE), BF16),
        pltpu.VMEM((FRAW, PAIRS, LANE), F32),
        pltpu.VMEM((6, BLK, LANE), F32),
    ]
    return pl.pallas_call(
        functools.partial(step_kernel, stages),
        out_shape=jax.ShapeDtypeStruct((3, BLK * LANE), F32),
        in_specs=[SMEM, SMEM, SMEM, VMEM, ANY, ANY, ANY, ANY],
        out_specs=VMEM,
        scratch_shapes=scratch,
        compiler_params=pltpu.CompilerParams(collective_id=0, has_side_effects=True, vmem_limit_bytes=56 * 1024 * 1024),
        name="step",
    )(jnp.transpose(send_list, (2, 0, 1)), pair_list, pair_count, pair_list, nodes, links, burgers, mobility)


def solution(mesh):
    return jax.shard_map(
        local,
        mesh=mesh,
        in_specs=(
            P(None, ("gx", "yz")),
            P(None, ("gx", "yz")),
            P(None, ("gx", "yz")),
            P(None, None, ("gx", "yz")),
            P(("gx", "yz"), None, None),
            P(None, ("gx", "yz")),
            P(("gx", "yz")),
        ),
        out_specs=P(None, ("gx", "yz")),
        check_vma=False,
    )
```

```python
import functools
import itertools
import math

import jax
import jax.numpy as jnp
from jax import lax
from jax.experimental import pallas as pl
from jax.experimental.pallas import tpu as pltpu
from jax.sharding import PartitionSpec as P

F32 = jnp.float32
BF16 = jnp.bfloat16
A_SQUARED = 0.25
NU_FACTOR = 0.4
DX_LIMIT = 1.0
SPEED_EPS = 1e-05
DIRECTIONS = ((-1, -1), (-1, 0), (-1, 1), (0, -1), (0, 1), (1, -1), (1, 0), (1, 1))
BLK = 32
LANE = 128
GB = 6
SLOTS = BLK + 64
QRAW = 8
FRAW = 24
CONV = 16
QK = 6 * QRAW
UNROLL = 40
SCAT = 16
PAIRS = 160
PSTRIDE = PAIRS + 8
MESH_ID = pl.DeviceIdType.MESH
STAGES = ((("yz", 1, 2),), (("gx", 1, 4), ("yz", 2, 4)), (("gx", 4, 4), ("yz", 8, 4)))


def cross(u, v):
    return [u[1] * v[2] - u[2] * v[1], u[2] * v[0] - u[0] * v[2], u[0] * v[1] - u[1] * v[0]]


def dot3(u, v):
    return u[0] * v[0] + u[1] * v[1] + u[2] * v[2]


def rounded(x):
    return x.astype(BF16).astype(F32)


def split2(x):
    high = rounded(x)
    return high, rounded(x - high)


def split3(x):
    high = rounded(x)
    rest = x - high
    mid = rounded(rest)
    return high, mid, rounded(rest - mid)


def to_rows(src_ref, rows, stage_ref, lead=None):
    for k in range(BLK):
        lanes = pl.ds(k * LANE, LANE)
        piece = src_ref[:, lanes] if lead is None else src_ref[lead, :, lanes]
        stage_ref[8 * k : 8 * k + rows, :] = piece
    return [stage_ref[pl.ds(c, BLK, stride=8), :] for c in range(rows)]


def gather_ends(table_ref, ends):
    outs = []
    for end in ends:
        high = end >> 7
        low = end & 127
        picked = [jnp.zeros((BLK, LANE), F32) for _ in range(3)]
        for row in range(BLK):
            here = high == row
            for c in range(3):
                wide = jnp.broadcast_to(table_ref[c, row : row + 1, :], (BLK, LANE))
                found = jnp.take_along_axis(wide, low, axis=1, mode="promise_in_bounds")
                picked[c] = jnp.where(here, found, picked[c])
        outs.append(picked)
    return outs


def pack_blocks(send_list, block_ref, rows, send_ref):
    for k in range(8):
        for g in range(GB):
            chosen = send_list[g, 0, k]
            send_ref[k, rows * g : rows * (g + 1), :] = block_ref[chosen, 0:rows, :]


def digits(stage):
    place = {"gx": lax.axis_index("gx"), "yz": lax.axis_index("yz")}
    found = []
    for offsets in itertools.product(*[range(size) for _, _, size in stage]):
        if any(offsets):
            peer = dict(place)
            for (axis, stride, size), offset in zip(stage, offsets):
                digit = lax.rem(lax.div(place[axis], stride), size)
                peer[axis] = peer[axis] + (lax.rem(digit + offset, size) - digit) * stride
            found.append((peer["gx"], peer["yz"]))
    return found


def neighbours():
    gx = lax.axis_index("gx")
    yz = lax.axis_index("yz")
    n_gx = lax.axis_size("gx")
    n_yz = lax.axis_size("yz")
    return [(lax.rem(gx + dx + n_gx, n_gx), lax.rem(yz + dy + n_yz, n_yz)) for dx, dy in DIRECTIONS]


def remote(source, target, send_sem, recv_sem, device):
    return pltpu.make_async_remote_copy(
        src_ref=source, dst_ref=target, send_sem=send_sem, recv_sem=recv_sem, device_id=device, device_id_type=MESH_ID
    )


def ghost_copies(send_ref, recv_ref, send_sem, recv_sem, targets):
    return [remote(send_ref.at[k], recv_ref.at[k], send_sem.at[k], recv_sem.at[k], targets[k]) for k in range(8)]


def put_rows(ref, slot, height, values):
    for row, value in enumerate(values):
        if value is not None:
            ref[pl.ds(slot * height + row, BLK, stride=height), :] = value


def filled(value):
    return jnp.full((BLK, LANE), value, F32)


def spread_features(order, slot, mid, line, burg, slope, q_refs, f_refs):
    moment = cross(burg, mid)
    if order == 0:
        put_rows(q_refs[0], slot, QRAW, mid + [dot3(mid, mid) + A_SQUARED, filled(1.0)] + [filled(0.0)] * 3)
        put_rows(f_refs[0], slot, FRAW, [line[a] * burg[d] for a in range(3) for d in range(3)])
        put_rows(f_refs[0], slot, FRAW, [None] * 9 + [line[a] * moment[d] for a in range(3) for d in range(3)])
        return
    mid_v, line_v = slope
    moment_v = cross(burg, mid_v)
    put_rows(q_refs[1], slot, QRAW, mid_v + [2.0 * dot3(mid, mid_v), dot3(mid_v, mid_v)] + [filled(0.0)] * 3)
    put_rows(f_refs[1], slot, FRAW, [line_v[a] * burg[d] for a in range(3) for d in range(3)])
    put_rows(
        f_refs[1], slot, FRAW,
        [None] * 9 + [line[a] * moment_v[d] + line_v[a] * moment[d] for a in range(3) for d in range(3)],
    )
    put_rows(f_refs[2], slot, FRAW, [filled(0.0)] * 9 + [line_v[a] * moment_v[d] for a in range(3) for d in range(3)])


def over_slots(own, ghosts, body):
    def own_trip(trip, carry):
        for j in range(CONV):
            body(CONV * trip + j)
        return carry

    def ghost_trip(trip, carry):
        for j in range(GB):
            body(BLK + 8 * trip + j)
        return carry

    if own:
        lax.fori_loop(0, BLK // CONV, own_trip, 0)
    if ghosts:
        lax.fori_loop(0, 8, ghost_trip, 0)


def turn_sources(order, own, ghosts, q_refs, qs_b):
    def body(slot):
        rows = pl.ds(pl.multiple_of(slot * QRAW, 8), QRAW)
        high, mid, low = split3(q_refs[order][rows, :])
        turned = jnp.transpose(jnp.concatenate([high, high, mid, mid, high, low], axis=0)).astype(BF16)
        qs_b[slot, :, QK * order : QK * (order + 1)] = turned

    over_slots(own, ghosts, body)


def convert_features(own, ghosts, step, f_refs, f_b):
    def body(slot):
        rows = pl.ds(pl.multiple_of(slot * FRAW, 8), FRAW)
        value = f_refs[0][rows, :]
        if step is not None:
            value = value + step * (f_refs[1][rows, :] + step * f_refs[2][rows, :])
        high, low = split2(value)
        part = jnp.concatenate([high, low], axis=0).astype(BF16)
        f_b[slot, :, 0:LANE] = part
        f_b[slot, :, LANE : 2 * LANE] = part

    over_slots(own, ghosts, body)


def convert_targets(mid, step, t_refs, qt_b):
    put_rows(t_refs[0], 0, QRAW, [-2.0 * mid[c] for c in range(3)] + [filled(1.0), dot3(mid, mid)] + [filled(0.0)] * 3)
    orders = 1
    if step is not None:
        orders = 2
        flat = filled(1.0) * step
        put_rows(t_refs[1], 0, QRAW, [-2.0 * step * mid[c] for c in range(3)] + [flat, step * flat] + [filled(0.0)] * 3)

    def body(trip, carry):
        for j in range(CONV):
            slot = CONV * trip + j
            for order in range(orders):
                high, mid_part, low = split3(t_refs[order][pl.ds(pl.multiple_of(slot * QRAW, 8), QRAW), :])
                qt_b[slot, QK * order : QK * (order + 1), :] = jnp.concatenate(
                    [high, mid_part, high, mid_part, low, high], axis=0
                ).astype(BF16)
        return carry

    lax.fori_loop(0, BLK // CONV, body, 0)


def pair_sums(depth, mid, line, burg, pairs, pair_row, count, ends_ref, mob_ref, qs_b, qt_b, f_b, acc, force_ref):
    def pair_step(step, carry):
        for j in range(UNROLL):
            place = UNROLL * step + j
            target = jnp.minimum(pairs[0, place], BLK - 1)
            source = pairs[1, place]
            ghost_place = source - BLK
            group = (ghost_place * 43) >> 8
            slot = jnp.where(source < BLK, source, BLK + 8 * group + (ghost_place - GB * group))
            dist = jnp.dot(qs_b[slot, :, 0:depth], qt_b[target, 0:depth, :], preferred_element_type=F32)
            root = lax.rsqrt(dist)
            weight = root * root * root
            high = weight.astype(BF16)
            low = (weight - high.astype(F32)).astype(BF16)
            both = jnp.concatenate([high, low], axis=0)
            found = jnp.dot(f_b[slot], both, preferred_element_type=F32)
            acc[pl.ds(place, FRAW, stride=PSTRIDE), :] = found[0:FRAW] + found[FRAW : 2 * FRAW]
        return carry

    lax.fori_loop(0, PAIRS // UNROLL, pair_step, 0)
    pair_id = lax.broadcasted_iota(jnp.int32, (BLK, PAIRS), 1)
    block_id = lax.broadcasted_iota(jnp.int32, (BLK, PAIRS), 0)
    chosen = jnp.where((block_id == pair_row[0:1, :]) & (pair_id < count), 1.0, 0.0).astype(BF16)
    chosen = jnp.concatenate([chosen, chosen], axis=1)

    def total(row):
        part = acc[PSTRIDE * row : PSTRIDE * row + PAIRS, :]
        high = part.astype(BF16)
        low = (part - high.astype(F32)).astype(BF16)
        return jnp.dot(chosen, jnp.concatenate([high, low], axis=0), preferred_element_type=F32)

    s_mat = [[total(3 * a + d) for d in range(3)] for a in range(3)]
    t_mat = [[total(9 + 3 * a + d) for d in range(3)] for a in range(3)]
    arm = cross(mid, burg)
    lined_s = [burg[0] * s_mat[0][d] + burg[1] * s_mat[1][d] + burg[2] * s_mat[2][d] for d in range(3)]
    lined_t = [burg[0] * t_mat[0][d] + burg[1] * t_mat[1][d] + burg[2] * t_mat[2][d] for d in range(3)]
    swept = cross(lined_s, mid)
    skew = [s_mat[2][1] - s_mat[1][2], s_mat[0][2] - s_mat[2][0], s_mat[1][0] - s_mat[0][1]]
    twist = NU_FACTOR * (dot3(mid, skew) + (t_mat[0][0] + t_mat[1][1] + t_mat[2][2]))
    traction = [
        0.5 * ((dot3(s_mat[k], arm) - dot3(t_mat[k], burg)) + (swept[k] - lined_t[k])) + twist * burg[k]
        for k in range(3)
    ]
    force = cross(traction, line)
    for c in range(3):
        high, low = split2(0.5 * force[c])
        force_ref[2 * c] = high
        force_ref[2 * c + 1] = low

    row_id = lax.broadcasted_iota(jnp.int32, (BLK, LANE), 0)
    lane_id = lax.broadcasted_iota(jnp.int32, (LANE, LANE), 0)

    def scatter_step(step, nodal):
        lhs = []
        rhs = []
        for j in range(SCAT):
            k = SCAT * step + j
            for e in range(2):
                end = ends_ref[e, pl.ds(k, 1), :]
                here = row_id == (end >> 7)
                lhs.append(
                    jnp.concatenate(
                        [jnp.where(here, force_ref[i, pl.ds(k, 1), :], 0.0).astype(BF16) for i in range(6)], axis=0
                    )
                )
                rhs.append(jnp.where(lane_id == (end & 127), 1.0, 0.0).astype(BF16))
        return nodal + lax.dot_general(
            jnp.concatenate(lhs, axis=1),
            jnp.concatenate(rhs, axis=1),
            (((1,), (1,)), ((), ())),
            preferred_element_type=F32,
        )

    nodal = lax.fori_loop(0, BLK // SCAT, scatter_step, jnp.zeros((6 * BLK, LANE), F32))
    pulled = [nodal[2 * BLK * c : 2 * BLK * c + BLK] + nodal[2 * BLK * c + BLK : 2 * BLK * (c + 1)] for c in range(3)]
    return [dot3([mob_ref[3 * r + c] for c in range(3)], pulled) for r in range(3)]


def step_kernel(
    stages, send_list_hbm, pairs_hbm, count_hbm, nodes_hbm, links_hbm, burgers_hbm, mobility_hbm, out_ref,
    nodes_ref, links_ref, burgers_ref, mobility_ref, send_list, pairs, count_ref, pair_row, in_sem,
    own_ref, own_v_ref, v_ref, ends_ref, mob_ref, ghost_ref, ghost_v_ref, stage_ref, block_ref,
    send_ref, recv_ref, send_v_ref, recv_v_ref, box_ref, mid_ref, gs1, gr1, gs2, gr2, ms, mr,
    q0_ref, q1_ref, f0_ref, f1_ref, f2_ref, t0_ref, t1_ref, qs_b, qt_b, f_b, acc, force_ref
):
    loads = [
        pltpu.make_async_copy(src, dst, in_sem.at[i])
        for i, (src, dst) in enumerate(
            (
                (nodes_hbm, nodes_ref),
                (links_hbm, links_ref),
                (burgers_hbm, burgers_ref),
                (send_list_hbm, send_list),
                (mobility_hbm, mobility_ref),
                (pairs_hbm, pairs),
                (pairs_hbm, pair_row),
                (count_hbm, count_ref),
            )
        )
    ]
    for load in loads:
        load.start()
    targets = neighbours()
    lines = [digits(stage) for stage in stages]
    peers = targets + [peer for line in lines for peer in line]
    barrier = pltpu.get_barrier_semaphore()
    for peer in peers:
        pl.semaphore_signal(barrier, inc=1, device_id=peer, device_id_type=MESH_ID)

    loads[0].wait()
    coords = to_rows(nodes_ref, 3, stage_ref)
    for c in range(3):
        v_ref[c] = coords[c]
    loads[1].wait()
    for k in range(BLK):
        lanes = pl.ds(k * LANE, LANE)
        ends_ref[0, k : k + 1, :] = links_ref[0:1, lanes]
        ends_ref[1, k : k + 1, :] = links_ref[1:2, lanes]
    first, second = gather_ends(v_ref, [ends_ref[0], ends_ref[1]])
    loads[2].wait()
    rows = [0.5 * (first[c] + second[c]) for c in range(3)] + [second[c] - first[c] for c in range(3)]
    rows = rows + to_rows(burgers_ref, 3, stage_ref)
    for c in range(9):
        own_ref[c] = rows[c]
        for k in range(BLK):
            block_ref[k, c : c + 1, :] = rows[c][k : k + 1]
    loads[3].wait()
    pack_blocks(send_list, block_ref, 9, send_ref)
    pl.semaphore_wait(barrier, len(peers))
    copies = ghost_copies(send_ref, recv_ref, gs1, gr1, targets)
    for copy in copies:
        copy.start()
    for load in loads[4:]:
        load.wait()
    count = count_ref[0]
    for r in range(3):
        rows = to_rows(mobility_ref, 3, stage_ref, r)
        for c in range(3):
            mob_ref[3 * r + c] = rows[c]

    q_refs = (q0_ref, q1_ref)
    t_refs = (t0_ref, t1_ref)
    f_refs = (f0_ref, f1_ref, f2_ref)
    tables = (qs_b, qt_b, f_b, acc, force_ref)
    own = [own_ref[c] for c in range(9)]
    centre = [jnp.mean(own[c]) for c in range(3)]
    mid = [own[c] - centre[c] for c in range(3)]
    spread_features(0, 0, mid, own[3:6], own[6:9], None, q_refs, f_refs)
    turn_sources(0, True, False, q_refs, qs_b)
    convert_features(True, False, None, f_refs, f_b)
    convert_targets(mid, None, t_refs, qt_b)
    for copy in copies:
        copy.wait_recv()
    for c in range(9):
        for k in range(8):
            ghost_ref[c, 8 * k : 8 * k + GB, :] = recv_ref[k, pl.ds(c, GB, stride=9), :]
            ghost_ref[c, 8 * k + GB : 8 * k + 8, :] = jnp.zeros((8 - GB, LANE), F32)
            if c < 6:
                ghost_v_ref[c, 8 * k + GB : 8 * k + 8, :] = jnp.zeros((8 - GB, LANE), F32)

    def ghost(half):
        rows = [ghost_ref[c, BLK * half : BLK * (half + 1), :] for c in range(9)]
        return [rows[c] - centre[c] for c in range(3)], rows[3:6], rows[6:9]

    for half in range(2):
        spread_features(0, BLK * (half + 1), *ghost(half), None, q_refs, f_refs)
    turn_sources(0, False, True, q_refs, qs_b)
    convert_features(False, True, None, f_refs, f_b)
    speed = pair_sums(QK, mid, own[3:6], own[6:9], pairs, pair_row, count, ends_ref, mob_ref, *tables)
    best = jnp.max(dot3(speed, speed), axis=0, keepdims=True)
    waiting = []

    def spread(stage, value):
        base = sum(len(line) for line in lines[:stage])
        mid_ref[stage] = value
        sent = [
            remote(mid_ref.at[stage], box_ref.at[base + o], ms.at[base + o], mr.at[base + o], peer)
            for o, peer in enumerate(lines[stage])
        ]
        for copy in sent:
            copy.start()
        waiting.extend(sent)
        return base, sent

    def settle(state, value):
        base, sent = state
        for copy in sent:
            copy.wait_recv()
        for o in range(len(sent)):
            value = jnp.maximum(value, box_ref[base + o])
        return value

    state = spread(0, best)
    for c in range(3):
        v_ref[c] = speed[c]
    best = settle(state, best)
    state = spread(1, best)
    first, second = gather_ends(v_ref, [ends_ref[0], ends_ref[1]])
    rows = [0.5 * (first[c] + second[c]) for c in range(3)] + [second[c] - first[c] for c in range(3)]
    for c in range(6):
        own_v_ref[c] = rows[c]
        for k in range(BLK):
            block_ref[k, c : c + 1, :] = rows[c][k : k + 1]
    pack_blocks(send_list, block_ref, 6, send_v_ref)
    copies_v = ghost_copies(send_v_ref, recv_v_ref, gs2, gr2, targets)
    for copy in copies_v:
        copy.start()
    best = settle(state, best)
    state = spread(2, best)
    own = [own_ref[c] for c in range(9)]
    mid = [own[c] - centre[c] for c in range(3)]
    own_v = [own_v_ref[c] for c in range(6)]
    spread_features(1, 0, mid, own[3:6], own[6:9], (own_v[0:3], own_v[3:6]), q_refs, f_refs)
    turn_sources(1, True, False, q_refs, qs_b)
    for copy in copies_v:
        copy.wait_recv()
    for c in range(6):
        for k in range(8):
            ghost_v_ref[c, 8 * k : 8 * k + GB, :] = recv_v_ref[k, pl.ds(c, GB, stride=6), :]
    for half in range(2):
        moving = [ghost_v_ref[c, BLK * half : BLK * (half + 1), :] for c in range(6)]
        spread_features(1, BLK * (half + 1), *ghost(half), (moving[0:3], moving[3:6]), q_refs, f_refs)
    turn_sources(1, False, True, q_refs, qs_b)
    best = settle(state, best)
    step = DX_LIMIT / (jnp.sqrt(jnp.max(best)) + SPEED_EPS)
    convert_features(True, True, step, f_refs, f_b)
    mid = [mid[c] + step * own_v[c] for c in range(3)]
    line = [own[3 + c] + step * own_v[3 + c] for c in range(3)]
    convert_targets(mid, step, t_refs, qt_b)
    speed = pair_sums(2 * QK, mid, line, own[6:9], pairs, pair_row, count, ends_ref, mob_ref, *tables)
    for c in range(3):
        stage_ref[pl.ds(c, BLK, stride=8), :] = 0.5 * step * (v_ref[c] + speed[c])
    for k in range(BLK):
        out_ref[:, pl.ds(k * LANE, LANE)] = stage_ref[8 * k : 8 * k + 3, :]
    for copy in copies + copies_v + waiting:
        copy.wait_send()


VMEM = pl.BlockSpec(memory_space=pltpu.VMEM)
HBM = pl.BlockSpec(memory_space=pltpu.HBM)
DMA = pltpu.SemaphoreType.DMA


def local(nodes, links, burgers, mobility, send_list, pair_list, pair_count):
    n_gx = lax.axis_size("gx")
    n_yz = lax.axis_size("yz")
    stages = STAGES
    mail = sum(math.prod(size for _, _, size in stage) - 1 for stage in stages)
    scratch = [
        pltpu.VMEM((3, BLK * LANE), F32),
        pltpu.VMEM((2, BLK * LANE), jnp.int32),
        pltpu.VMEM((3, BLK * LANE), F32),
        pltpu.VMEM((3, 3, BLK * LANE), F32),
        pltpu.SMEM((GB, 1, 8), jnp.int32),
        pltpu.SMEM((2, PAIRS), jnp.int32),
        pltpu.SMEM((1,), jnp.int32),
        pltpu.VMEM((2, PAIRS), jnp.int32),
        DMA((8,)),
        pltpu.VMEM((9, BLK, LANE), F32),
        pltpu.VMEM((6, BLK, LANE), F32),
        pltpu.VMEM((3, BLK, LANE), F32),
        pltpu.VMEM((2, BLK, LANE), jnp.int32),
        pltpu.VMEM((9, BLK, LANE), F32),
        pltpu.VMEM((9, 64, LANE), F32),
        pltpu.VMEM((6, 64, LANE), F32),
        pltpu.VMEM((BLK * 8, LANE), F32),
        pltpu.VMEM((BLK, 16, LANE), F32),
        pltpu.VMEM((8, 9 * GB, LANE), F32),
        pltpu.VMEM((8, 9 * GB, LANE), F32),
        pltpu.VMEM((8, 6 * GB, LANE), F32),
        pltpu.VMEM((8, 6 * GB, LANE), F32),
        pltpu.VMEM((mail, 1, LANE), F32),
        pltpu.VMEM((len(stages), 1, LANE), F32),
        DMA((8,)), DMA((8,)), DMA((8,)), DMA((8,)), DMA((mail,)), DMA((mail,)),
        *[pltpu.VMEM((SLOTS * QRAW, LANE), F32)] * 2,
        *[pltpu.VMEM((SLOTS * FRAW, LANE), F32)] * 3,
        *[pltpu.VMEM((BLK * QRAW, LANE), F32)] * 2,
        pltpu.VMEM((SLOTS, LANE, 2 * QK), BF16),
        pltpu.VMEM((BLK, 2 * QK, LANE), BF16),
        pltpu.VMEM((SLOTS, 2 * FRAW, 2 * LANE), BF16),
        pltpu.VMEM((FRAW * PSTRIDE, LANE), F32),
        pltpu.VMEM((6, BLK, LANE), F32),
    ]
    return pl.pallas_call(
        functools.partial(step_kernel, stages),
        out_shape=jax.ShapeDtypeStruct((3, BLK * LANE), F32),
        in_specs=[HBM] * 7,
        out_specs=VMEM,
        scratch_shapes=scratch,
        compiler_params=pltpu.CompilerParams(collective_id=0, has_side_effects=True, vmem_limit_bytes=56 * 1024 * 1024),
        name="step",
    )(jnp.transpose(send_list, (2, 0, 1)), pair_list, pair_count, nodes, links, burgers, mobility)


def solution(mesh):
    return jax.shard_map(
        local,
        mesh=mesh,
        in_specs=(
            P(None, ("gx", "yz")),
            P(None, ("gx", "yz")),
            P(None, ("gx", "yz")),
            P(None, None, ("gx", "yz")),
            P(("gx", "yz"), None, None),
            P(None, ("gx", "yz")),
            P(("gx", "yz")),
        ),
        out_specs=P(None, ("gx", "yz")),
        check_vma=False,
    )
```

```python
import functools
import itertools
import math

import jax
import jax.numpy as jnp
from jax import lax
from jax.experimental import pallas as pl
from jax.experimental.pallas import tpu as pltpu
from jax.sharding import PartitionSpec as P

F32 = jnp.float32
BF16 = jnp.bfloat16
A_SQUARED = 0.25
NU_FACTOR = 0.4
DX_LIMIT = 1.0
SPEED_EPS = 1e-05
DIRECTIONS = ((-1, -1), (-1, 0), (-1, 1), (0, -1), (0, 1), (1, -1), (1, 0), (1, 1))
BLK = 32
LANE = 128
GB = 6
SLOTS = BLK + 64
QRAW = 8
FRAW = 24
CONV = 16
QK = 6 * QRAW
UNROLL = 80
SCAT = 16
PAIRS = 160
PSTRIDE = PAIRS + 8
MESH_ID = pl.DeviceIdType.MESH
STAGES = ((("yz", 1, 2),), (("gx", 1, 4), ("yz", 2, 4)), (("gx", 4, 4), ("yz", 8, 4)))


def cross(u, v):
    return [u[1] * v[2] - u[2] * v[1], u[2] * v[0] - u[0] * v[2], u[0] * v[1] - u[1] * v[0]]


def dot3(u, v):
    return u[0] * v[0] + u[1] * v[1] + u[2] * v[2]


def rounded(x):
    return x.astype(BF16).astype(F32)


def split2(x):
    high = rounded(x)
    return high, rounded(x - high)


def split3(x):
    high = rounded(x)
    rest = x - high
    mid = rounded(rest)
    return high, mid, rounded(rest - mid)


def to_rows(src_ref, rows, stage_ref, lead=None):
    for k in range(BLK):
        lanes = pl.ds(k * LANE, LANE)
        piece = src_ref[:, lanes] if lead is None else src_ref[lead, :, lanes]
        stage_ref[8 * k : 8 * k + rows, :] = piece
    return [stage_ref[pl.ds(c, BLK, stride=8), :] for c in range(rows)]


def gather_ends(table_ref, ends):
    outs = []
    for end in ends:
        high = end >> 7
        low = end & 127
        picked = [jnp.zeros((BLK, LANE), F32) for _ in range(3)]
        for row in range(BLK):
            here = high == row
            for c in range(3):
                wide = jnp.broadcast_to(table_ref[c, row : row + 1, :], (BLK, LANE))
                found = jnp.take_along_axis(wide, low, axis=1, mode="promise_in_bounds")
                picked[c] = jnp.where(here, found, picked[c])
        outs.append(picked)
    return outs


def pack_blocks(send_list, block_ref, rows, send_ref):
    for k in range(8):
        for g in range(GB):
            chosen = send_list[g, 0, k]
            send_ref[k, rows * g : rows * (g + 1), :] = block_ref[chosen, 0:rows, :]


def digits(stage):
    place = {"gx": lax.axis_index("gx"), "yz": lax.axis_index("yz")}
    found = []
    for offsets in itertools.product(*[range(size) for _, _, size in stage]):
        if any(offsets):
            peer = dict(place)
            for (axis, stride, size), offset in zip(stage, offsets):
                digit = lax.rem(lax.div(place[axis], stride), size)
                peer[axis] = peer[axis] + (lax.rem(digit + offset, size) - digit) * stride
            found.append((peer["gx"], peer["yz"]))
    return found


def neighbours():
    gx = lax.axis_index("gx")
    yz = lax.axis_index("yz")
    n_gx = lax.axis_size("gx")
    n_yz = lax.axis_size("yz")
    return [(lax.rem(gx + dx + n_gx, n_gx), lax.rem(yz + dy + n_yz, n_yz)) for dx, dy in DIRECTIONS]


def remote(source, target, send_sem, recv_sem, device):
    return pltpu.make_async_remote_copy(
        src_ref=source, dst_ref=target, send_sem=send_sem, recv_sem=recv_sem, device_id=device, device_id_type=MESH_ID
    )


def ghost_copies(send_ref, recv_ref, send_sem, recv_sem, targets):
    return [remote(send_ref.at[k], recv_ref.at[k], send_sem.at[k], recv_sem.at[k], targets[k]) for k in range(8)]


def put_rows(ref, slot, height, values):
    for row, value in enumerate(values):
        if value is not None:
            ref[pl.ds(slot * height + row, BLK, stride=height), :] = value


def filled(value):
    return jnp.full((BLK, LANE), value, F32)


def spread_features(order, slot, mid, line, burg, slope, q_refs, f_refs):
    moment = cross(burg, mid)
    if order == 0:
        put_rows(q_refs[0], slot, QRAW, mid + [dot3(mid, mid) + A_SQUARED, filled(1.0)] + [filled(0.0)] * 3)
        put_rows(f_refs[0], slot, FRAW, [line[a] * burg[d] for a in range(3) for d in range(3)])
        put_rows(f_refs[0], slot, FRAW, [None] * 9 + [line[a] * moment[d] for a in range(3) for d in range(3)])
        return
    mid_v, line_v = slope
    moment_v = cross(burg, mid_v)
    put_rows(q_refs[1], slot, QRAW, mid_v + [2.0 * dot3(mid, mid_v), dot3(mid_v, mid_v)] + [filled(0.0)] * 3)
    put_rows(f_refs[1], slot, FRAW, [line_v[a] * burg[d] for a in range(3) for d in range(3)])
    put_rows(
        f_refs[1], slot, FRAW,
        [None] * 9 + [line[a] * moment_v[d] + line_v[a] * moment[d] for a in range(3) for d in range(3)],
    )
    put_rows(f_refs[2], slot, FRAW, [filled(0.0)] * 9 + [line_v[a] * moment_v[d] for a in range(3) for d in range(3)])


def over_slots(own, ghosts, body):
    def own_trip(trip, carry):
        for j in range(CONV):
            body(CONV * trip + j)
        return carry

    def ghost_trip(trip, carry):
        for j in range(GB):
            body(BLK + 8 * trip + j)
        return carry

    if own:
        lax.fori_loop(0, BLK // CONV, own_trip, 0)
    if ghosts:
        lax.fori_loop(0, 8, ghost_trip, 0)


def turn_sources(order, own, ghosts, q_refs, qs_b):
    def body(slot):
        rows = pl.ds(pl.multiple_of(slot * QRAW, 8), QRAW)
        high, mid, low = split3(q_refs[order][rows, :])
        turned = jnp.transpose(jnp.concatenate([high, high, mid, mid, high, low], axis=0)).astype(BF16)
        qs_b[slot, :, QK * order : QK * (order + 1)] = turned

    over_slots(own, ghosts, body)


def convert_features(own, ghosts, step, f_refs, f_b):
    def body(slot):
        rows = pl.ds(pl.multiple_of(slot * FRAW, 8), FRAW)
        value = f_refs[0][rows, :]
        if step is not None:
            value = value + step * (f_refs[1][rows, :] + step * f_refs[2][rows, :])
        high, low = split2(value)
        part = jnp.concatenate([high, low], axis=0).astype(BF16)
        f_b[slot, :, 0:LANE] = part
        f_b[slot, :, LANE : 2 * LANE] = part

    over_slots(own, ghosts, body)


def convert_targets(mid, step, t_refs, qt_b):
    put_rows(t_refs[0], 0, QRAW, [-2.0 * mid[c] for c in range(3)] + [filled(1.0), dot3(mid, mid)] + [filled(0.0)] * 3)
    orders = 1
    if step is not None:
        orders = 2
        flat = filled(1.0) * step
        put_rows(t_refs[1], 0, QRAW, [-2.0 * step * mid[c] for c in range(3)] + [flat, step * flat] + [filled(0.0)] * 3)

    def body(trip, carry):
        for j in range(CONV):
            slot = CONV * trip + j
            for order in range(orders):
                high, mid_part, low = split3(t_refs[order][pl.ds(pl.multiple_of(slot * QRAW, 8), QRAW), :])
                qt_b[slot, QK * order : QK * (order + 1), :] = jnp.concatenate(
                    [high, mid_part, high, mid_part, low, high], axis=0
                ).astype(BF16)
        return carry

    lax.fori_loop(0, BLK // CONV, body, 0)


def pair_sums(depth, mid, line, burg, pairs, pair_row, count, ends_ref, mob_ref, qs_b, qt_b, f_b, acc, force_ref):
    def pair_step(step, carry):
        for j in range(UNROLL):
            place = UNROLL * step + j
            target = jnp.minimum(pairs[0, place], BLK - 1)
            source = pairs[1, place]
            ghost_place = source - BLK
            group = (ghost_place * 43) >> 8
            slot = jnp.where(source < BLK, source, BLK + 8 * group + (ghost_place - GB * group))
            dist = jnp.dot(qs_b[slot, :, 0:depth], qt_b[target, 0:depth, :], preferred_element_type=F32)
            root = lax.rsqrt(dist)
            weight = root * root * root
            high = weight.astype(BF16)
            low = (weight - high.astype(F32)).astype(BF16)
            both = jnp.concatenate([high, low], axis=0)
            found = jnp.dot(f_b[slot], both, preferred_element_type=F32)
            acc[pl.ds(place, FRAW, stride=PSTRIDE), :] = found[0:FRAW] + found[FRAW : 2 * FRAW]
        return carry

    lax.fori_loop(0, PAIRS // UNROLL, pair_step, 0)
    pair_id = lax.broadcasted_iota(jnp.int32, (BLK, PAIRS), 1)
    block_id = lax.broadcasted_iota(jnp.int32, (BLK, PAIRS), 0)
    chosen = jnp.where((block_id == pair_row[0:1, :]) & (pair_id < count), 1.0, 0.0).astype(BF16)
    chosen = jnp.concatenate([chosen, chosen], axis=1)

    def total(row):
        part = acc[PSTRIDE * row : PSTRIDE * row + PAIRS, :]
        high = part.astype(BF16)
        low = (part - high.astype(F32)).astype(BF16)
        return jnp.dot(chosen, jnp.concatenate([high, low], axis=0), preferred_element_type=F32)

    s_mat = [[total(3 * a + d) for d in range(3)] for a in range(3)]
    t_mat = [[total(9 + 3 * a + d) for d in range(3)] for a in range(3)]
    arm = cross(mid, burg)
    lined_s = [burg[0] * s_mat[0][d] + burg[1] * s_mat[1][d] + burg[2] * s_mat[2][d] for d in range(3)]
    lined_t = [burg[0] * t_mat[0][d] + burg[1] * t_mat[1][d] + burg[2] * t_mat[2][d] for d in range(3)]
    swept = cross(lined_s, mid)
    skew = [s_mat[2][1] - s_mat[1][2], s_mat[0][2] - s_mat[2][0], s_mat[1][0] - s_mat[0][1]]
    twist = NU_FACTOR * (dot3(mid, skew) + (t_mat[0][0] + t_mat[1][1] + t_mat[2][2]))
    traction = [
        0.5 * ((dot3(s_mat[k], arm) - dot3(t_mat[k], burg)) + (swept[k] - lined_t[k])) + twist * burg[k]
        for k in range(3)
    ]
    force = cross(traction, line)
    for c in range(3):
        high, low = split2(0.5 * force[c])
        force_ref[2 * c] = high
        force_ref[2 * c + 1] = low

    row_id = lax.broadcasted_iota(jnp.int32, (BLK, LANE), 0)
    lane_id = lax.broadcasted_iota(jnp.int32, (LANE, LANE), 0)

    def scatter_step(step, nodal):
        lhs = []
        rhs = []
        for j in range(SCAT):
            k = SCAT * step + j
            for e in range(2):
                end = ends_ref[e, pl.ds(k, 1), :]
                here = row_id == (end >> 7)
                lhs.append(
                    jnp.concatenate(
                        [jnp.where(here, force_ref[i, pl.ds(k, 1), :], 0.0).astype(BF16) for i in range(6)], axis=0
                    )
                )
                rhs.append(jnp.where(lane_id == (end & 127), 1.0, 0.0).astype(BF16))
        return nodal + lax.dot_general(
            jnp.concatenate(lhs, axis=1),
            jnp.concatenate(rhs, axis=1),
            (((1,), (1,)), ((), ())),
            preferred_element_type=F32,
        )

    nodal = lax.fori_loop(0, BLK // SCAT, scatter_step, jnp.zeros((6 * BLK, LANE), F32))
    pulled = [nodal[2 * BLK * c : 2 * BLK * c + BLK] + nodal[2 * BLK * c + BLK : 2 * BLK * (c + 1)] for c in range(3)]
    return [dot3([mob_ref[3 * r + c] for c in range(3)], pulled) for r in range(3)]


def step_kernel(
    stages, send_list_hbm, pairs_hbm, count_hbm, nodes_hbm, links_hbm, burgers_hbm, mobility_hbm, out_ref,
    nodes_ref, links_ref, burgers_ref, mobility_ref, send_list, pairs, count_ref, pair_row, in_sem,
    own_ref, own_v_ref, v_ref, ends_ref, mob_ref, ghost_ref, ghost_v_ref, stage_ref, block_ref,
    send_ref, recv_ref, send_v_ref, recv_v_ref, box_ref, mid_ref, gs1, gr1, gs2, gr2, ms, mr,
    q0_ref, q1_ref, f0_ref, f1_ref, f2_ref, t0_ref, t1_ref, qs_b, qt_b, f_b, acc, force_ref
):
    loads = [
        pltpu.make_async_copy(src, dst, in_sem.at[i])
        for i, (src, dst) in enumerate(
            (
                (nodes_hbm, nodes_ref),
                (links_hbm, links_ref),
                (burgers_hbm, burgers_ref),
                (send_list_hbm, send_list),
                (mobility_hbm, mobility_ref),
                (pairs_hbm, pairs),
                (pairs_hbm, pair_row),
                (count_hbm, count_ref),
            )
        )
    ]
    for load in loads:
        load.start()
    targets = neighbours()
    lines = [digits(stage) for stage in stages]
    peers = targets + [peer for line in lines for peer in line]
    barrier = pltpu.get_barrier_semaphore()
    for peer in peers:
        pl.semaphore_signal(barrier, inc=1, device_id=peer, device_id_type=MESH_ID)

    loads[0].wait()
    coords = to_rows(nodes_ref, 3, stage_ref)
    for c in range(3):
        v_ref[c] = coords[c]
    loads[1].wait()
    for k in range(BLK):
        lanes = pl.ds(k * LANE, LANE)
        ends_ref[0, k : k + 1, :] = links_ref[0:1, lanes]
        ends_ref[1, k : k + 1, :] = links_ref[1:2, lanes]
    first, second = gather_ends(v_ref, [ends_ref[0], ends_ref[1]])
    loads[2].wait()
    rows = [0.5 * (first[c] + second[c]) for c in range(3)] + [second[c] - first[c] for c in range(3)]
    rows = rows + to_rows(burgers_ref, 3, stage_ref)
    for c in range(9):
        own_ref[c] = rows[c]
        for k in range(BLK):
            block_ref[k, c : c + 1, :] = rows[c][k : k + 1]
    loads[3].wait()
    pack_blocks(send_list, block_ref, 9, send_ref)
    pl.semaphore_wait(barrier, len(peers))
    copies = ghost_copies(send_ref, recv_ref, gs1, gr1, targets)
    for copy in copies:
        copy.start()
    for load in loads[4:]:
        load.wait()
    count = count_ref[0]
    for r in range(3):
        rows = to_rows(mobility_ref, 3, stage_ref, r)
        for c in range(3):
            mob_ref[3 * r + c] = rows[c]

    q_refs = (q0_ref, q1_ref)
    t_refs = (t0_ref, t1_ref)
    f_refs = (f0_ref, f1_ref, f2_ref)
    tables = (qs_b, qt_b, f_b, acc, force_ref)
    own = [own_ref[c] for c in range(9)]
    centre = [jnp.mean(own[c]) for c in range(3)]
    mid = [own[c] - centre[c] for c in range(3)]
    spread_features(0, 0, mid, own[3:6], own[6:9], None, q_refs, f_refs)
    turn_sources(0, True, False, q_refs, qs_b)
    convert_features(True, False, None, f_refs, f_b)
    convert_targets(mid, None, t_refs, qt_b)
    for copy in copies:
        copy.wait_recv()
    for c in range(9):
        for k in range(8):
            ghost_ref[c, 8 * k : 8 * k + GB, :] = recv_ref[k, pl.ds(c, GB, stride=9), :]
            ghost_ref[c, 8 * k + GB : 8 * k + 8, :] = jnp.zeros((8 - GB, LANE), F32)
            if c < 6:
                ghost_v_ref[c, 8 * k + GB : 8 * k + 8, :] = jnp.zeros((8 - GB, LANE), F32)

    def ghost(half):
        rows = [ghost_ref[c, BLK * half : BLK * (half + 1), :] for c in range(9)]
        return [rows[c] - centre[c] for c in range(3)], rows[3:6], rows[6:9]

    for half in range(2):
        spread_features(0, BLK * (half + 1), *ghost(half), None, q_refs, f_refs)
    turn_sources(0, False, True, q_refs, qs_b)
    convert_features(False, True, None, f_refs, f_b)
    speed = pair_sums(QK, mid, own[3:6], own[6:9], pairs, pair_row, count, ends_ref, mob_ref, *tables)
    best = jnp.max(dot3(speed, speed), axis=0, keepdims=True)
    waiting = []

    def spread(stage, value):
        base = sum(len(line) for line in lines[:stage])
        mid_ref[stage] = value
        sent = [
            remote(mid_ref.at[stage], box_ref.at[base + o], ms.at[base + o], mr.at[base + o], peer)
            for o, peer in enumerate(lines[stage])
        ]
        for copy in sent:
            copy.start()
        waiting.extend(sent)
        return base, sent

    def settle(state, value):
        base, sent = state
        for copy in sent:
            copy.wait_recv()
        for o in range(len(sent)):
            value = jnp.maximum(value, box_ref[base + o])
        return value

    state = spread(0, best)
    for c in range(3):
        v_ref[c] = speed[c]
    best = settle(state, best)
    state = spread(1, best)
    first, second = gather_ends(v_ref, [ends_ref[0], ends_ref[1]])
    rows = [0.5 * (first[c] + second[c]) for c in range(3)] + [second[c] - first[c] for c in range(3)]
    for c in range(6):
        own_v_ref[c] = rows[c]
        for k in range(BLK):
            block_ref[k, c : c + 1, :] = rows[c][k : k + 1]
    pack_blocks(send_list, block_ref, 6, send_v_ref)
    copies_v = ghost_copies(send_v_ref, recv_v_ref, gs2, gr2, targets)
    for copy in copies_v:
        copy.start()
    best = settle(state, best)
    state = spread(2, best)
    own = [own_ref[c] for c in range(9)]
    mid = [own[c] - centre[c] for c in range(3)]
    own_v = [own_v_ref[c] for c in range(6)]
    spread_features(1, 0, mid, own[3:6], own[6:9], (own_v[0:3], own_v[3:6]), q_refs, f_refs)
    turn_sources(1, True, False, q_refs, qs_b)
    for copy in copies_v:
        copy.wait_recv()
    for c in range(6):
        for k in range(8):
            ghost_v_ref[c, 8 * k : 8 * k + GB, :] = recv_v_ref[k, pl.ds(c, GB, stride=6), :]
    for half in range(2):
        moving = [ghost_v_ref[c, BLK * half : BLK * (half + 1), :] for c in range(6)]
        spread_features(1, BLK * (half + 1), *ghost(half), (moving[0:3], moving[3:6]), q_refs, f_refs)
    turn_sources(1, False, True, q_refs, qs_b)
    best = settle(state, best)
    step = DX_LIMIT / (jnp.sqrt(jnp.max(best)) + SPEED_EPS)
    convert_features(True, True, step, f_refs, f_b)
    mid = [mid[c] + step * own_v[c] for c in range(3)]
    line = [own[3 + c] + step * own_v[3 + c] for c in range(3)]
    convert_targets(mid, step, t_refs, qt_b)
    speed = pair_sums(2 * QK, mid, line, own[6:9], pairs, pair_row, count, ends_ref, mob_ref, *tables)
    for c in range(3):
        stage_ref[pl.ds(c, BLK, stride=8), :] = 0.5 * step * (v_ref[c] + speed[c])
    for k in range(BLK):
        out_ref[:, pl.ds(k * LANE, LANE)] = stage_ref[8 * k : 8 * k + 3, :]
    for copy in copies + copies_v + waiting:
        copy.wait_send()


VMEM = pl.BlockSpec(memory_space=pltpu.VMEM)
HBM = pl.BlockSpec(memory_space=pltpu.HBM)
DMA = pltpu.SemaphoreType.DMA


def local(nodes, links, burgers, mobility, send_list, pair_list, pair_count):
    n_gx = lax.axis_size("gx")
    n_yz = lax.axis_size("yz")
    stages = STAGES
    mail = sum(math.prod(size for _, _, size in stage) - 1 for stage in stages)
    scratch = [
        pltpu.VMEM((3, BLK * LANE), F32),
        pltpu.VMEM((2, BLK * LANE), jnp.int32),
        pltpu.VMEM((3, BLK * LANE), F32),
        pltpu.VMEM((3, 3, BLK * LANE), F32),
        pltpu.SMEM((GB, 1, 8), jnp.int32),
        pltpu.SMEM((2, PAIRS), jnp.int32),
        pltpu.SMEM((1,), jnp.int32),
        pltpu.VMEM((2, PAIRS), jnp.int32),
        DMA((8,)),
        pltpu.VMEM((9, BLK, LANE), F32),
        pltpu.VMEM((6, BLK, LANE), F32),
        pltpu.VMEM((3, BLK, LANE), F32),
        pltpu.VMEM((2, BLK, LANE), jnp.int32),
        pltpu.VMEM((9, BLK, LANE), F32),
        pltpu.VMEM((9, 64, LANE), F32),
        pltpu.VMEM((6, 64, LANE), F32),
        pltpu.VMEM((BLK * 8, LANE), F32),
        pltpu.VMEM((BLK, 16, LANE), F32),
        pltpu.VMEM((8, 9 * GB, LANE), F32),
        pltpu.VMEM((8, 9 * GB, LANE), F32),
        pltpu.VMEM((8, 6 * GB, LANE), F32),
        pltpu.VMEM((8, 6 * GB, LANE), F32),
        pltpu.VMEM((mail, 1, LANE), F32),
        pltpu.VMEM((len(stages), 1, LANE), F32),
        DMA((8,)), DMA((8,)), DMA((8,)), DMA((8,)), DMA((mail,)), DMA((mail,)),
        *[pltpu.VMEM((SLOTS * QRAW, LANE), F32)] * 2,
        *[pltpu.VMEM((SLOTS * FRAW, LANE), F32)] * 3,
        *[pltpu.VMEM((BLK * QRAW, LANE), F32)] * 2,
        pltpu.VMEM((SLOTS, LANE, 2 * QK), BF16),
        pltpu.VMEM((BLK, 2 * QK, LANE), BF16),
        pltpu.VMEM((SLOTS, 2 * FRAW, 2 * LANE), BF16),
        pltpu.VMEM((FRAW * PSTRIDE, LANE), F32),
        pltpu.VMEM((6, BLK, LANE), F32),
    ]
    return pl.pallas_call(
        functools.partial(step_kernel, stages),
        out_shape=pltpu.VMEM((3, BLK * LANE), F32),
        in_specs=[HBM] * 7,
        out_specs=VMEM,
        scratch_shapes=scratch,
        compiler_params=pltpu.CompilerParams(collective_id=0, has_side_effects=True, vmem_limit_bytes=56 * 1024 * 1024),
        name="step",
    )(jnp.transpose(send_list, (2, 0, 1)), pair_list, pair_count, nodes, links, burgers, mobility)


def solution(mesh):
    return jax.shard_map(
        local,
        mesh=mesh,
        in_specs=(
            P(None, ("gx", "yz")),
            P(None, ("gx", "yz")),
            P(None, ("gx", "yz")),
            P(None, None, ("gx", "yz")),
            P(("gx", "yz"), None, None),
            P(None, ("gx", "yz")),
            P(("gx", "yz")),
        ),
        out_specs=P(None, ("gx", "yz")),
        check_vma=False,
    )
```

```python
import functools
import itertools
import math

import jax
import jax.numpy as jnp
from jax import lax
from jax.experimental import pallas as pl
from jax.experimental.pallas import tpu as pltpu
from jax.sharding import PartitionSpec as P

F32 = jnp.float32
BF16 = jnp.bfloat16
A_SQUARED = 0.25
NU_FACTOR = 0.4
DX_LIMIT = 1.0
SPEED_EPS = 1e-05
DIRECTIONS = ((-1, -1), (-1, 0), (-1, 1), (0, -1), (0, 1), (1, -1), (1, 0), (1, 1))
BLK = 32
LANE = 128
GB = 6
SLOTS = BLK + 64
QRAW = 8
FRAW = 24
CONV = 32
GTRIP = 8
QK = 6 * QRAW
UNROLL = 160
SCAT = 32
PAIRS = 160
PSTRIDE = PAIRS + 8
MESH_ID = pl.DeviceIdType.MESH
STAGES = ((("yz", 1, 2),), (("gx", 1, 4), ("yz", 2, 4)), (("gx", 4, 4), ("yz", 8, 4)))


def cross(u, v):
    return [u[1] * v[2] - u[2] * v[1], u[2] * v[0] - u[0] * v[2], u[0] * v[1] - u[1] * v[0]]


def dot3(u, v):
    return u[0] * v[0] + u[1] * v[1] + u[2] * v[2]


def rounded(x):
    return x.astype(BF16).astype(F32)


def split2(x):
    high = rounded(x)
    return high, rounded(x - high)


def split3(x):
    high = rounded(x)
    rest = x - high
    mid = rounded(rest)
    return high, mid, rounded(rest - mid)


def to_rows(src_ref, rows, stage_ref, lead=None):
    for k in range(BLK):
        lanes = pl.ds(k * LANE, LANE)
        piece = src_ref[:, lanes] if lead is None else src_ref[lead, :, lanes]
        stage_ref[8 * k : 8 * k + rows, :] = piece
    return [stage_ref[pl.ds(c, BLK, stride=8), :] for c in range(rows)]


def gather_ends(table_ref, ends):
    outs = []
    for end in ends:
        high = end >> 7
        low = end & 127
        picked = [jnp.zeros((BLK, LANE), F32) for _ in range(3)]
        for row in range(BLK):
            here = high == row
            for c in range(3):
                wide = jnp.broadcast_to(table_ref[c, row : row + 1, :], (BLK, LANE))
                found = jnp.take_along_axis(wide, low, axis=1, mode="promise_in_bounds")
                picked[c] = jnp.where(here, found, picked[c])
        outs.append(picked)
    return outs


def pack_blocks(send_list, block_ref, rows, send_ref):
    for k in range(8):
        for g in range(GB):
            chosen = send_list[g, 0, k]
            send_ref[k, rows * g : rows * (g + 1), :] = block_ref[chosen, 0:rows, :]


def digits(stage):
    place = {"gx": lax.axis_index("gx"), "yz": lax.axis_index("yz")}
    found = []
    for offsets in itertools.product(*[range(size) for _, _, size in stage]):
        if any(offsets):
            peer = dict(place)
            for (axis, stride, size), offset in zip(stage, offsets):
                digit = lax.rem(lax.div(place[axis], stride), size)
                peer[axis] = peer[axis] + (lax.rem(digit + offset, size) - digit) * stride
            found.append((peer["gx"], peer["yz"]))
    return found


def neighbours():
    gx = lax.axis_index("gx")
    yz = lax.axis_index("yz")
    n_gx = lax.axis_size("gx")
    n_yz = lax.axis_size("yz")
    return [(lax.rem(gx + dx + n_gx, n_gx), lax.rem(yz + dy + n_yz, n_yz)) for dx, dy in DIRECTIONS]


def remote(source, target, send_sem, recv_sem, device):
    return pltpu.make_async_remote_copy(
        src_ref=source, dst_ref=target, send_sem=send_sem, recv_sem=recv_sem, device_id=device, device_id_type=MESH_ID
    )


def ghost_copies(send_ref, recv_ref, send_sem, recv_sem, targets):
    return [remote(send_ref.at[k], recv_ref.at[k], send_sem.at[k], recv_sem.at[k], targets[k]) for k in range(8)]


def put_rows(ref, slot, height, values):
    for row, value in enumerate(values):
        if value is not None:
            ref[pl.ds(slot * height + row, BLK, stride=height), :] = value


def filled(value):
    return jnp.full((BLK, LANE), value, F32)


def spread_features(order, slot, mid, line, burg, slope, q_refs, f_refs):
    moment = cross(burg, mid)
    if order == 0:
        put_rows(q_refs[0], slot, QRAW, mid + [dot3(mid, mid) + A_SQUARED, filled(1.0)] + [filled(0.0)] * 3)
        put_rows(f_refs[0], slot, FRAW, [line[a] * burg[d] for a in range(3) for d in range(3)])
        put_rows(f_refs[0], slot, FRAW, [None] * 9 + [line[a] * moment[d] for a in range(3) for d in range(3)])
        return
    mid_v, line_v = slope
    moment_v = cross(burg, mid_v)
    put_rows(q_refs[1], slot, QRAW, mid_v + [2.0 * dot3(mid, mid_v), dot3(mid_v, mid_v)] + [filled(0.0)] * 3)
    put_rows(f_refs[1], slot, FRAW, [line_v[a] * burg[d] for a in range(3) for d in range(3)])
    put_rows(
        f_refs[1], slot, FRAW,
        [None] * 9 + [line[a] * moment_v[d] + line_v[a] * moment[d] for a in range(3) for d in range(3)],
    )
    put_rows(f_refs[2], slot, FRAW, [filled(0.0)] * 9 + [line_v[a] * moment_v[d] for a in range(3) for d in range(3)])


def over_slots(own, ghosts, body):
    def own_trip(trip, carry):
        for j in range(CONV):
            body(CONV * trip + j)
        return carry

    def ghost_trip(trip, carry):
        for j in range(8 * GTRIP):
            if j % 8 < GB:
                body(BLK + 8 * GTRIP * trip + j)
        return carry

    if own:
        lax.fori_loop(0, BLK // CONV, own_trip, 0)
    if ghosts:
        lax.fori_loop(0, 8 // GTRIP, ghost_trip, 0)


def turn_sources(order, own, ghosts, q_refs, qs_b):
    def body(slot):
        rows = pl.ds(pl.multiple_of(slot * QRAW, 8), QRAW)
        high, mid, low = split3(q_refs[order][rows, :])
        turned = jnp.transpose(jnp.concatenate([high, high, mid, mid, high, low], axis=0).astype(BF16))
        qs_b[slot, :, QK * order : QK * (order + 1)] = turned

    over_slots(own, ghosts, body)


def convert_features(own, ghosts, step, f_refs, f_b):
    def body(slot):
        rows = pl.ds(pl.multiple_of(slot * FRAW, 8), FRAW)
        value = f_refs[0][rows, :]
        if step is not None:
            value = value + step * (f_refs[1][rows, :] + step * f_refs[2][rows, :])
        high, low = split2(value)
        part = jnp.concatenate([high, low], axis=0).astype(BF16)
        f_b[slot, :, 0:LANE] = part
        f_b[slot, :, LANE : 2 * LANE] = part

    over_slots(own, ghosts, body)


def convert_targets(mid, step, t_refs, qt_b):
    put_rows(t_refs[0], 0, QRAW, [-2.0 * mid[c] for c in range(3)] + [filled(1.0), dot3(mid, mid)] + [filled(0.0)] * 3)
    orders = 1
    if step is not None:
        orders = 2
        flat = filled(1.0) * step
        put_rows(t_refs[1], 0, QRAW, [-2.0 * step * mid[c] for c in range(3)] + [flat, step * flat] + [filled(0.0)] * 3)

    def body(trip, carry):
        for j in range(CONV):
            slot = CONV * trip + j
            for order in range(orders):
                high, mid_part, low = split3(t_refs[order][pl.ds(pl.multiple_of(slot * QRAW, 8), QRAW), :])
                qt_b[slot, QK * order : QK * (order + 1), :] = jnp.concatenate(
                    [high, mid_part, high, mid_part, low, high], axis=0
                ).astype(BF16)
        return carry

    lax.fori_loop(0, BLK // CONV, body, 0)


def pair_sums(depth, mid, line, burg, pairs, pair_row, count, ends_ref, mob_ref, qs_b, qt_b, f_b, acc, force_ref):
    def pair_step(step, carry):
        for j in range(UNROLL):
            place = UNROLL * step + j
            target = jnp.minimum(pairs[0, place], BLK - 1)
            source = pairs[1, place]
            ghost_place = source - BLK
            group = (ghost_place * 43) >> 8
            slot = jnp.where(source < BLK, source, BLK + 8 * group + (ghost_place - GB * group))
            dist = jnp.dot(qs_b[slot, :, 0:depth], qt_b[target, 0:depth, :], preferred_element_type=F32)
            root = lax.rsqrt(dist)
            weight = root * root * root
            high = weight.astype(BF16)
            low = (weight - high.astype(F32)).astype(BF16)
            both = jnp.concatenate([high, low], axis=0)
            found = jnp.dot(f_b[slot], both, preferred_element_type=F32)
            acc[pl.ds(place, FRAW, stride=PSTRIDE), :] = found[0:FRAW] + found[FRAW : 2 * FRAW]
        return carry

    lax.fori_loop(0, PAIRS // UNROLL, pair_step, 0)
    pair_id = lax.broadcasted_iota(jnp.int32, (BLK, PAIRS), 1)
    block_id = lax.broadcasted_iota(jnp.int32, (BLK, PAIRS), 0)
    chosen = jnp.where((block_id == pair_row[0:1, :]) & (pair_id < count), 1.0, 0.0).astype(BF16)
    chosen = jnp.concatenate([chosen, chosen], axis=1)

    def total(row):
        part = acc[PSTRIDE * row : PSTRIDE * row + PAIRS, :]
        high = part.astype(BF16)
        low = (part - high.astype(F32)).astype(BF16)
        return jnp.dot(chosen, jnp.concatenate([high, low], axis=0), preferred_element_type=F32)

    s_mat = [[total(3 * a + d) for d in range(3)] for a in range(3)]
    t_mat = [[total(9 + 3 * a + d) for d in range(3)] for a in range(3)]
    arm = cross(mid, burg)
    lined_s = [burg[0] * s_mat[0][d] + burg[1] * s_mat[1][d] + burg[2] * s_mat[2][d] for d in range(3)]
    lined_t = [burg[0] * t_mat[0][d] + burg[1] * t_mat[1][d] + burg[2] * t_mat[2][d] for d in range(3)]
    swept = cross(lined_s, mid)
    skew = [s_mat[2][1] - s_mat[1][2], s_mat[0][2] - s_mat[2][0], s_mat[1][0] - s_mat[0][1]]
    twist = NU_FACTOR * (dot3(mid, skew) + (t_mat[0][0] + t_mat[1][1] + t_mat[2][2]))
    traction = [
        0.5 * ((dot3(s_mat[k], arm) - dot3(t_mat[k], burg)) + (swept[k] - lined_t[k])) + twist * burg[k]
        for k in range(3)
    ]
    force = cross(traction, line)
    for c in range(3):
        high, low = split2(0.5 * force[c])
        force_ref[2 * c] = high
        force_ref[2 * c + 1] = low

    row_id = lax.broadcasted_iota(jnp.int32, (BLK, LANE), 0)
    lane_id = lax.broadcasted_iota(jnp.int32, (LANE, LANE), 0)

    def scatter_step(step, nodal):
        lhs = []
        rhs = []
        for j in range(SCAT):
            k = SCAT * step + j
            for e in range(2):
                end = ends_ref[e, pl.ds(k, 1), :]
                here = row_id == (end >> 7)
                lhs.append(
                    jnp.concatenate(
                        [jnp.where(here, force_ref[i, pl.ds(k, 1), :], 0.0).astype(BF16) for i in range(6)], axis=0
                    )
                )
                rhs.append(jnp.where(lane_id == (end & 127), 1.0, 0.0).astype(BF16))
        return nodal + lax.dot_general(
            jnp.concatenate(lhs, axis=1),
            jnp.concatenate(rhs, axis=1),
            (((1,), (1,)), ((), ())),
            preferred_element_type=F32,
        )

    nodal = lax.fori_loop(0, BLK // SCAT, scatter_step, jnp.zeros((6 * BLK, LANE), F32))
    pulled = [nodal[2 * BLK * c : 2 * BLK * c + BLK] + nodal[2 * BLK * c + BLK : 2 * BLK * (c + 1)] for c in range(3)]
    return [dot3([mob_ref[3 * r + c] for c in range(3)], pulled) for r in range(3)]


def step_kernel(
    stages, send_list_hbm, pairs_hbm, count_hbm, nodes_hbm, links_hbm, burgers_hbm, mobility_hbm, out_ref,
    nodes_ref, links_ref, burgers_ref, mobility_ref, send_list, pairs, count_ref, pair_row, in_sem,
    own_ref, own_v_ref, v_ref, ends_ref, mob_ref, ghost_ref, ghost_v_ref, stage_ref, block_ref,
    send_ref, recv_ref, send_v_ref, recv_v_ref, box_ref, mid_ref, gs1, gr1, gs2, gr2, ms, mr,
    q0_ref, q1_ref, f0_ref, f1_ref, f2_ref, t0_ref, t1_ref, qs_b, qt_b, f_b, acc, force_ref
):
    loads = [
        pltpu.make_async_copy(src, dst, in_sem.at[i])
        for i, (src, dst) in enumerate(
            (
                (nodes_hbm, nodes_ref),
                (links_hbm, links_ref),
                (burgers_hbm, burgers_ref),
                (send_list_hbm, send_list),
                (mobility_hbm, mobility_ref),
                (pairs_hbm, pairs),
                (pairs_hbm, pair_row),
                (count_hbm, count_ref),
            )
        )
    ]
    for load in loads:
        load.start()
    targets = neighbours()
    lines = [digits(stage) for stage in stages]
    peers = targets + [peer for line in lines for peer in line]
    barrier = pltpu.get_barrier_semaphore()
    for peer in peers:
        pl.semaphore_signal(barrier, inc=1, device_id=peer, device_id_type=MESH_ID)

    loads[0].wait()
    coords = to_rows(nodes_ref, 3, stage_ref)
    for c in range(3):
        v_ref[c] = coords[c]
    loads[1].wait()
    for k in range(BLK):
        lanes = pl.ds(k * LANE, LANE)
        ends_ref[0, k : k + 1, :] = links_ref[0:1, lanes]
        ends_ref[1, k : k + 1, :] = links_ref[1:2, lanes]
    first, second = gather_ends(v_ref, [ends_ref[0], ends_ref[1]])
    loads[2].wait()
    rows = [0.5 * (first[c] + second[c]) for c in range(3)] + [second[c] - first[c] for c in range(3)]
    rows = rows + to_rows(burgers_ref, 3, stage_ref)
    for c in range(9):
        own_ref[c] = rows[c]
        for k in range(BLK):
            block_ref[k, c : c + 1, :] = rows[c][k : k + 1]
    loads[3].wait()
    pack_blocks(send_list, block_ref, 9, send_ref)
    pl.semaphore_wait(barrier, len(peers))
    copies = ghost_copies(send_ref, recv_ref, gs1, gr1, targets)
    for copy in copies:
        copy.start()
    for load in loads[4:]:
        load.wait()
    count = count_ref[0]
    for r in range(3):
        rows = to_rows(mobility_ref, 3, stage_ref, r)
        for c in range(3):
            mob_ref[3 * r + c] = rows[c]

    q_refs = (q0_ref, q1_ref)
    t_refs = (t0_ref, t1_ref)
    f_refs = (f0_ref, f1_ref, f2_ref)
    tables = (qs_b, qt_b, f_b, acc, force_ref)
    own = [own_ref[c] for c in range(9)]
    centre = [jnp.mean(own[c]) for c in range(3)]
    mid = [own[c] - centre[c] for c in range(3)]
    spread_features(0, 0, mid, own[3:6], own[6:9], None, q_refs, f_refs)
    turn_sources(0, True, False, q_refs, qs_b)
    convert_features(True, False, None, f_refs, f_b)
    convert_targets(mid, None, t_refs, qt_b)
    for copy in copies:
        copy.wait_recv()
    for c in range(9):
        for k in range(8):
            ghost_ref[c, 8 * k : 8 * k + GB, :] = recv_ref[k, pl.ds(c, GB, stride=9), :]
            ghost_ref[c, 8 * k + GB : 8 * k + 8, :] = jnp.zeros((8 - GB, LANE), F32)
            if c < 6:
                ghost_v_ref[c, 8 * k + GB : 8 * k + 8, :] = jnp.zeros((8 - GB, LANE), F32)

    def ghost(half):
        rows = [ghost_ref[c, BLK * half : BLK * (half + 1), :] for c in range(9)]
        return [rows[c] - centre[c] for c in range(3)], rows[3:6], rows[6:9]

    for half in range(2):
        spread_features(0, BLK * (half + 1), *ghost(half), None, q_refs, f_refs)
    turn_sources(0, False, True, q_refs, qs_b)
    convert_features(False, True, None, f_refs, f_b)
    speed = pair_sums(QK, mid, own[3:6], own[6:9], pairs, pair_row, count, ends_ref, mob_ref, *tables)
    best = jnp.max(dot3(speed, speed), axis=0, keepdims=True)
    waiting = []

    def spread(stage, value):
        base = sum(len(line) for line in lines[:stage])
        mid_ref[stage] = value
        sent = [
            remote(mid_ref.at[stage], box_ref.at[base + o], ms.at[base + o], mr.at[base + o], peer)
            for o, peer in enumerate(lines[stage])
        ]
        for copy in sent:
            copy.start()
        waiting.extend(sent)
        return base, sent

    def settle(state, value):
        base, sent = state
        for copy in sent:
            copy.wait_recv()
        for o in range(len(sent)):
            value = jnp.maximum(value, box_ref[base + o])
        return value

    state = spread(0, best)
    for c in range(3):
        v_ref[c] = speed[c]
    best = settle(state, best)
    state = spread(1, best)
    first, second = gather_ends(v_ref, [ends_ref[0], ends_ref[1]])
    rows = [0.5 * (first[c] + second[c]) for c in range(3)] + [second[c] - first[c] for c in range(3)]
    for c in range(6):
        own_v_ref[c] = rows[c]
        for k in range(BLK):
            block_ref[k, c : c + 1, :] = rows[c][k : k + 1]
    pack_blocks(send_list, block_ref, 6, send_v_ref)
    copies_v = ghost_copies(send_v_ref, recv_v_ref, gs2, gr2, targets)
    for copy in copies_v:
        copy.start()
    best = settle(state, best)
    state = spread(2, best)
    own = [own_ref[c] for c in range(9)]
    mid = [own[c] - centre[c] for c in range(3)]
    own_v = [own_v_ref[c] for c in range(6)]
    spread_features(1, 0, mid, own[3:6], own[6:9], (own_v[0:3], own_v[3:6]), q_refs, f_refs)
    turn_sources(1, True, False, q_refs, qs_b)
    for copy in copies_v:
        copy.wait_recv()
    for c in range(6):
        for k in range(8):
            ghost_v_ref[c, 8 * k : 8 * k + GB, :] = recv_v_ref[k, pl.ds(c, GB, stride=6), :]
    for half in range(2):
        moving = [ghost_v_ref[c, BLK * half : BLK * (half + 1), :] for c in range(6)]
        spread_features(1, BLK * (half + 1), *ghost(half), (moving[0:3], moving[3:6]), q_refs, f_refs)
    turn_sources(1, False, True, q_refs, qs_b)
    best = settle(state, best)
    step = DX_LIMIT / (jnp.sqrt(jnp.max(best)) + SPEED_EPS)
    convert_features(True, True, step, f_refs, f_b)
    mid = [mid[c] + step * own_v[c] for c in range(3)]
    line = [own[3 + c] + step * own_v[3 + c] for c in range(3)]
    convert_targets(mid, step, t_refs, qt_b)
    speed = pair_sums(2 * QK, mid, line, own[6:9], pairs, pair_row, count, ends_ref, mob_ref, *tables)
    for c in range(3):
        stage_ref[pl.ds(c, BLK, stride=8), :] = 0.5 * step * (v_ref[c] + speed[c])
    for k in range(BLK):
        out_ref[:, pl.ds(k * LANE, LANE)] = stage_ref[8 * k : 8 * k + 3, :]
    for copy in copies + copies_v + waiting:
        copy.wait_send()


VMEM = pl.BlockSpec(memory_space=pltpu.VMEM)
HBM = pl.BlockSpec(memory_space=pltpu.HBM)
DMA = pltpu.SemaphoreType.DMA


def local(nodes, links, burgers, mobility, send_list, pair_list, pair_count):
    n_gx = lax.axis_size("gx")
    n_yz = lax.axis_size("yz")
    stages = STAGES
    mail = sum(math.prod(size for _, _, size in stage) - 1 for stage in stages)
    scratch = [
        pltpu.VMEM((3, BLK * LANE), F32),
        pltpu.VMEM((2, BLK * LANE), jnp.int32),
        pltpu.VMEM((3, BLK * LANE), F32),
        pltpu.VMEM((3, 3, BLK * LANE), F32),
        pltpu.SMEM((GB, 1, 8), jnp.int32),
        pltpu.SMEM((2, PAIRS), jnp.int32),
        pltpu.SMEM((1,), jnp.int32),
        pltpu.VMEM((2, PAIRS), jnp.int32),
        DMA((8,)),
        pltpu.VMEM((9, BLK, LANE), F32),
        pltpu.VMEM((6, BLK, LANE), F32),
        pltpu.VMEM((3, BLK, LANE), F32),
        pltpu.VMEM((2, BLK, LANE), jnp.int32),
        pltpu.VMEM((9, BLK, LANE), F32),
        pltpu.VMEM((9, 64, LANE), F32),
        pltpu.VMEM((6, 64, LANE), F32),
        pltpu.VMEM((BLK * 8, LANE), F32),
        pltpu.VMEM((BLK, 16, LANE), F32),
        pltpu.VMEM((8, 9 * GB, LANE), F32),
        pltpu.VMEM((8, 9 * GB, LANE), F32),
        pltpu.VMEM((8, 6 * GB, LANE), F32),
        pltpu.VMEM((8, 6 * GB, LANE), F32),
        pltpu.VMEM((mail, 1, LANE), F32),
        pltpu.VMEM((len(stages), 1, LANE), F32),
        DMA((8,)), DMA((8,)), DMA((8,)), DMA((8,)), DMA((mail,)), DMA((mail,)),
        *[pltpu.VMEM((SLOTS * QRAW, LANE), F32)] * 2,
        *[pltpu.VMEM((SLOTS * FRAW, LANE), F32)] * 3,
        *[pltpu.VMEM((BLK * QRAW, LANE), F32)] * 2,
        pltpu.VMEM((SLOTS, LANE, 2 * QK), BF16),
        pltpu.VMEM((BLK, 2 * QK, LANE), BF16),
        pltpu.VMEM((SLOTS, 2 * FRAW, 2 * LANE), BF16),
        pltpu.VMEM((FRAW * PSTRIDE, LANE), F32),
        pltpu.VMEM((6, BLK, LANE), F32),
    ]
    return pl.pallas_call(
        functools.partial(step_kernel, stages),
        out_shape=pltpu.VMEM((3, BLK * LANE), F32),
        in_specs=[HBM] * 7,
        out_specs=VMEM,
        scratch_shapes=scratch,
        compiler_params=pltpu.CompilerParams(collective_id=0, has_side_effects=True, vmem_limit_bytes=56 * 1024 * 1024),
        name="step",
    )(jnp.transpose(send_list, (2, 0, 1)), pair_list, pair_count, nodes, links, burgers, mobility)


def solution(mesh):
    return jax.shard_map(
        local,
        mesh=mesh,
        in_specs=(
            P(None, ("gx", "yz")),
            P(None, ("gx", "yz")),
            P(None, ("gx", "yz")),
            P(None, None, ("gx", "yz")),
            P(("gx", "yz"), None, None),
            P(None, ("gx", "yz")),
            P(("gx", "yz")),
        ),
        out_specs=P(None, ("gx", "yz")),
        check_vma=False,
    )
```

```python
import functools
import itertools
import math

import jax
import jax.numpy as jnp
from jax import lax
from jax.experimental import pallas as pl
from jax.experimental.pallas import tpu as pltpu
from jax.sharding import PartitionSpec as P

F32 = jnp.float32
BF16 = jnp.bfloat16
A_SQUARED = 0.25
NU_FACTOR = 0.4
DX_LIMIT = 1.0
SPEED_EPS = 1e-05
DIRECTIONS = ((-1, -1), (-1, 0), (-1, 1), (0, -1), (0, 1), (1, -1), (1, 0), (1, 1))
BLK = 32
LANE = 128
GB = 6
SLOTS = BLK + 64
QRAW = 8
FRAW = 24
CONV = 16
GTRIP = 2
QK = 6 * QRAW
UNROLL = 80
SCAT = 16
PAIRS = 160
PSTRIDE = PAIRS + 8
MESH_ID = pl.DeviceIdType.MESH
STAGES = ((("yz", 1, 2),), (("gx", 1, 4), ("yz", 2, 4)), (("gx", 4, 4), ("yz", 8, 4)))


def cross(u, v):
    return [u[1] * v[2] - u[2] * v[1], u[2] * v[0] - u[0] * v[2], u[0] * v[1] - u[1] * v[0]]


def dot3(u, v):
    return u[0] * v[0] + u[1] * v[1] + u[2] * v[2]


def rounded(x):
    return x.astype(BF16).astype(F32)


def split2(x):
    high = rounded(x)
    return high, rounded(x - high)


def split3(x):
    high = rounded(x)
    rest = x - high
    mid = rounded(rest)
    return high, mid, rounded(rest - mid)


def to_rows(src_ref, rows, stage_ref, lead=None):
    for k in range(BLK):
        lanes = pl.ds(k * LANE, LANE)
        piece = src_ref[:, lanes] if lead is None else src_ref[lead, :, lanes]
        stage_ref[8 * k : 8 * k + rows, :] = piece
    return [stage_ref[pl.ds(c, BLK, stride=8), :] for c in range(rows)]


def gather_ends(table_ref, ends):
    outs = []
    for end in ends:
        high = end >> 7
        low = end & 127
        picked = [jnp.zeros((BLK, LANE), F32) for _ in range(3)]
        for row in range(BLK):
            here = high == row
            for c in range(3):
                wide = jnp.broadcast_to(table_ref[c, row : row + 1, :], (BLK, LANE))
                found = jnp.take_along_axis(wide, low, axis=1, mode="promise_in_bounds")
                picked[c] = jnp.where(here, found, picked[c])
        outs.append(picked)
    return outs


def pack_blocks(send_list, block_ref, rows, send_ref):
    for k in range(8):
        for g in range(GB):
            chosen = send_list[g, 0, k]
            send_ref[k, rows * g : rows * (g + 1), :] = block_ref[chosen, 0:rows, :]


def digits(stage):
    place = {"gx": lax.axis_index("gx"), "yz": lax.axis_index("yz")}
    found = []
    for offsets in itertools.product(*[range(size) for _, _, size in stage]):
        if any(offsets):
            peer = dict(place)
            for (axis, stride, size), offset in zip(stage, offsets):
                digit = lax.rem(lax.div(place[axis], stride), size)
                peer[axis] = peer[axis] + (lax.rem(digit + offset, size) - digit) * stride
            found.append((peer["gx"], peer["yz"]))
    return found


def neighbours():
    gx = lax.axis_index("gx")
    yz = lax.axis_index("yz")
    n_gx = lax.axis_size("gx")
    n_yz = lax.axis_size("yz")
    return [(lax.rem(gx + dx + n_gx, n_gx), lax.rem(yz + dy + n_yz, n_yz)) for dx, dy in DIRECTIONS]


def remote(source, target, send_sem, recv_sem, device):
    return pltpu.make_async_remote_copy(
        src_ref=source, dst_ref=target, send_sem=send_sem, recv_sem=recv_sem, device_id=device, device_id_type=MESH_ID
    )


def ghost_copies(send_ref, recv_ref, send_sem, recv_sem, targets):
    return [remote(send_ref.at[k], recv_ref.at[k], send_sem.at[k], recv_sem.at[k], targets[k]) for k in range(8)]


def put_rows(ref, slot, height, values):
    for row, value in enumerate(values):
        if value is not None:
            ref[pl.ds(slot * height + row, BLK, stride=height), :] = value


def filled(value):
    return jnp.full((BLK, LANE), value, F32)


def spread_features(order, slot, mid, line, burg, slope, q_refs, f_refs):
    moment = cross(burg, mid)
    if order == 0:
        put_rows(q_refs[0], slot, QRAW, mid + [dot3(mid, mid) + A_SQUARED, filled(1.0)] + [filled(0.0)] * 3)
        put_rows(f_refs[0], slot, FRAW, [line[a] * burg[d] for a in range(3) for d in range(3)])
        put_rows(f_refs[0], slot, FRAW, [None] * 9 + [line[a] * moment[d] for a in range(3) for d in range(3)])
        return
    mid_v, line_v = slope
    moment_v = cross(burg, mid_v)
    put_rows(q_refs[1], slot, QRAW, mid_v + [2.0 * dot3(mid, mid_v), dot3(mid_v, mid_v)] + [filled(0.0)] * 3)
    put_rows(f_refs[1], slot, FRAW, [line_v[a] * burg[d] for a in range(3) for d in range(3)])
    put_rows(
        f_refs[1], slot, FRAW,
        [None] * 9 + [line[a] * moment_v[d] + line_v[a] * moment[d] for a in range(3) for d in range(3)],
    )
    put_rows(f_refs[2], slot, FRAW, [filled(0.0)] * 9 + [line_v[a] * moment_v[d] for a in range(3) for d in range(3)])


def over_slots(own, ghosts, body):
    def own_trip(trip, carry):
        for j in range(CONV):
            body(CONV * trip + j)
        return carry

    def ghost_trip(trip, carry):
        for j in range(8 * GTRIP):
            if j % 8 < GB:
                body(BLK + 8 * GTRIP * trip + j)
        return carry

    if own:
        lax.fori_loop(0, BLK // CONV, own_trip, 0)
    if ghosts:
        lax.fori_loop(0, 8 // GTRIP, ghost_trip, 0)


def turn_sources(order, own, ghosts, q_refs, qs_b):
    def body(slot):
        rows = pl.ds(pl.multiple_of(slot * QRAW, 8), QRAW)
        high, mid, low = split3(q_refs[order][rows, :])
        turned = jnp.transpose(jnp.concatenate([high, high, mid, mid, high, low], axis=0).astype(BF16))
        qs_b[slot, :, QK * order : QK * (order + 1)] = turned

    over_slots(own, ghosts, body)


def convert_features(own, ghosts, step, f_refs, f_b):
    def body(slot):
        rows = pl.ds(pl.multiple_of(slot * FRAW, 8), FRAW)
        value = f_refs[0][rows, :]
        if step is not None:
            value = value + step * (f_refs[1][rows, :] + step * f_refs[2][rows, :])
        high, low = split2(value)
        part = jnp.concatenate([high, low], axis=0).astype(BF16)
        f_b[slot, :, 0:LANE] = part
        f_b[slot, :, LANE : 2 * LANE] = part

    over_slots(own, ghosts, body)


def convert_targets(mid, step, t_refs, qt_b):
    put_rows(t_refs[0], 0, QRAW, [-2.0 * mid[c] for c in range(3)] + [filled(1.0), dot3(mid, mid)] + [filled(0.0)] * 3)
    orders = 1
    if step is not None:
        orders = 2
        flat = filled(1.0) * step
        put_rows(t_refs[1], 0, QRAW, [-2.0 * step * mid[c] for c in range(3)] + [flat, step * flat] + [filled(0.0)] * 3)

    def body(trip, carry):
        for j in range(CONV):
            slot = CONV * trip + j
            for order in range(orders):
                high, mid_part, low = split3(t_refs[order][pl.ds(pl.multiple_of(slot * QRAW, 8), QRAW), :])
                qt_b[slot, QK * order : QK * (order + 1), :] = jnp.concatenate(
                    [high, mid_part, high, mid_part, low, high], axis=0
                ).astype(BF16)
        return carry

    lax.fori_loop(0, BLK // CONV, body, 0)


def pair_sums(depth, mid, line, burg, pairs, pair_row, count, ends_ref, mob_ref, qs_b, qt_b, f_b, acc, force_ref):
    def pair_step(step, carry):
        for j in range(UNROLL):
            place = UNROLL * step + j
            target = jnp.minimum(pairs[0, place], BLK - 1)
            source = pairs[1, place]
            ghost_place = source - BLK
            group = (ghost_place * 43) >> 8
            slot = jnp.where(source < BLK, source, BLK + 8 * group + (ghost_place - GB * group))
            dist = jnp.dot(qs_b[slot, :, 0:depth], qt_b[target, 0:depth, :], preferred_element_type=F32)
            root = lax.rsqrt(dist)
            weight = root * root * root
            high = weight.astype(BF16)
            low = (weight - high.astype(F32)).astype(BF16)
            both = jnp.concatenate([high, low], axis=0)
            found = jnp.dot(f_b[slot], both, preferred_element_type=F32)
            acc[pl.ds(place, FRAW, stride=PSTRIDE), :] = found[0:FRAW] + found[FRAW : 2 * FRAW]
        return carry

    lax.fori_loop(0, PAIRS // UNROLL, pair_step, 0)
    pair_id = lax.broadcasted_iota(jnp.int32, (BLK, PAIRS), 1)
    block_id = lax.broadcasted_iota(jnp.int32, (BLK, PAIRS), 0)
    chosen = jnp.where((block_id == pair_row[0:1, :]) & (pair_id < count), 1.0, 0.0).astype(BF16)
    chosen = jnp.concatenate([chosen, chosen], axis=1)

    def total(row):
        part = acc[PSTRIDE * row : PSTRIDE * row + PAIRS, :]
        high = part.astype(BF16)
        low = (part - high.astype(F32)).astype(BF16)
        return jnp.dot(chosen, jnp.concatenate([high, low], axis=0), preferred_element_type=F32)

    s_mat = [[total(3 * a + d) for d in range(3)] for a in range(3)]
    t_mat = [[total(9 + 3 * a + d) for d in range(3)] for a in range(3)]
    arm = cross(mid, burg)
    lined_s = [burg[0] * s_mat[0][d] + burg[1] * s_mat[1][d] + burg[2] * s_mat[2][d] for d in range(3)]
    lined_t = [burg[0] * t_mat[0][d] + burg[1] * t_mat[1][d] + burg[2] * t_mat[2][d] for d in range(3)]
    swept = cross(lined_s, mid)
    skew = [s_mat[2][1] - s_mat[1][2], s_mat[0][2] - s_mat[2][0], s_mat[1][0] - s_mat[0][1]]
    twist = NU_FACTOR * (dot3(mid, skew) + (t_mat[0][0] + t_mat[1][1] + t_mat[2][2]))
    traction = [
        0.5 * ((dot3(s_mat[k], arm) - dot3(t_mat[k], burg)) + (swept[k] - lined_t[k])) + twist * burg[k]
        for k in range(3)
    ]
    force = cross(traction, line)
    for c in range(3):
        high, low = split2(0.5 * force[c])
        force_ref[2 * c] = high
        force_ref[2 * c + 1] = low

    row_id = lax.broadcasted_iota(jnp.int32, (BLK, LANE), 0)
    lane_id = lax.broadcasted_iota(jnp.int32, (LANE, LANE), 0)

    def scatter_step(step, nodal):
        lhs = []
        rhs = []
        for j in range(SCAT):
            k = SCAT * step + j
            for e in range(2):
                end = ends_ref[e, pl.ds(k, 1), :]
                here = row_id == (end >> 7)
                lhs.append(
                    jnp.concatenate(
                        [jnp.where(here, force_ref[i, pl.ds(k, 1), :], 0.0).astype(BF16) for i in range(6)], axis=0
                    )
                )
                rhs.append(jnp.where(lane_id == (end & 127), 1.0, 0.0).astype(BF16))
        return nodal + lax.dot_general(
            jnp.concatenate(lhs, axis=1),
            jnp.concatenate(rhs, axis=1),
            (((1,), (1,)), ((), ())),
            preferred_element_type=F32,
        )

    nodal = lax.fori_loop(0, BLK // SCAT, scatter_step, jnp.zeros((6 * BLK, LANE), F32))
    pulled = [nodal[2 * BLK * c : 2 * BLK * c + BLK] + nodal[2 * BLK * c + BLK : 2 * BLK * (c + 1)] for c in range(3)]
    return [dot3([mob_ref[3 * r + c] for c in range(3)], pulled) for r in range(3)]


def step_kernel(
    stages, send_list_hbm, pairs_hbm, count_hbm, nodes_hbm, links_hbm, burgers_hbm, mobility_hbm, out_ref,
    nodes_ref, links_ref, burgers_ref, mobility_ref, send_list, pairs, count_ref, pair_row, in_sem,
    own_ref, own_v_ref, v_ref, ends_ref, mob_ref, ghost_ref, ghost_v_ref, stage_ref, block_ref,
    send_ref, recv_ref, send_v_ref, recv_v_ref, box_ref, mid_ref, gs1, gr1, gs2, gr2, ms, mr,
    q0_ref, q1_ref, f0_ref, f1_ref, f2_ref, t0_ref, t1_ref, qs_b, qt_b, f_b, acc, force_ref
):
    loads = [
        pltpu.make_async_copy(src, dst, in_sem.at[i])
        for i, (src, dst) in enumerate(
            (
                (nodes_hbm, nodes_ref),
                (links_hbm, links_ref),
                (burgers_hbm, burgers_ref),
                (send_list_hbm, send_list),
                (mobility_hbm, mobility_ref),
                (pairs_hbm, pairs),
                (pairs_hbm, pair_row),
                (count_hbm, count_ref),
            )
        )
    ]
    for load in loads:
        load.start()
    targets = neighbours()
    lines = [digits(stage) for stage in stages]
    peers = targets + [peer for line in lines for peer in line]
    barrier = pltpu.get_barrier_semaphore()
    for peer in peers:
        pl.semaphore_signal(barrier, inc=1, device_id=peer, device_id_type=MESH_ID)

    loads[0].wait()
    coords = to_rows(nodes_ref, 3, stage_ref)
    for c in range(3):
        v_ref[c] = coords[c]
    loads[1].wait()
    for k in range(BLK):
        lanes = pl.ds(k * LANE, LANE)
        ends_ref[0, k : k + 1, :] = links_ref[0:1, lanes]
        ends_ref[1, k : k + 1, :] = links_ref[1:2, lanes]
    first, second = gather_ends(v_ref, [ends_ref[0], ends_ref[1]])
    loads[2].wait()
    rows = [0.5 * (first[c] + second[c]) for c in range(3)] + [second[c] - first[c] for c in range(3)]
    rows = rows + to_rows(burgers_ref, 3, stage_ref)
    for c in range(9):
        own_ref[c] = rows[c]
        for k in range(BLK):
            block_ref[k, c : c + 1, :] = rows[c][k : k + 1]
    loads[3].wait()
    pack_blocks(send_list, block_ref, 9, send_ref)
    pl.semaphore_wait(barrier, len(peers))
    copies = ghost_copies(send_ref, recv_ref, gs1, gr1, targets)
    for copy in copies:
        copy.start()
    for load in loads[4:]:
        load.wait()
    count = count_ref[0]
    for r in range(3):
        rows = to_rows(mobility_ref, 3, stage_ref, r)
        for c in range(3):
            mob_ref[3 * r + c] = rows[c]

    q_refs = (q0_ref, q1_ref)
    t_refs = (t0_ref, t1_ref)
    f_refs = (f0_ref, f1_ref, f2_ref)
    tables = (qs_b, qt_b, f_b, acc, force_ref)
    own = [own_ref[c] for c in range(9)]
    centre = [jnp.mean(own[c]) for c in range(3)]
    mid = [own[c] - centre[c] for c in range(3)]
    spread_features(0, 0, mid, own[3:6], own[6:9], None, q_refs, f_refs)
    turn_sources(0, True, False, q_refs, qs_b)
    convert_features(True, False, None, f_refs, f_b)
    convert_targets(mid, None, t_refs, qt_b)
    for copy in copies:
        copy.wait_recv()
    for c in range(9):
        for k in range(8):
            ghost_ref[c, 8 * k : 8 * k + GB, :] = recv_ref[k, pl.ds(c, GB, stride=9), :]
            ghost_ref[c, 8 * k + GB : 8 * k + 8, :] = jnp.zeros((8 - GB, LANE), F32)
            if c < 6:
                ghost_v_ref[c, 8 * k + GB : 8 * k + 8, :] = jnp.zeros((8 - GB, LANE), F32)

    def ghost(half):
        rows = [ghost_ref[c, BLK * half : BLK * (half + 1), :] for c in range(9)]
        return [rows[c] - centre[c] for c in range(3)], rows[3:6], rows[6:9]

    for half in range(2):
        spread_features(0, BLK * (half + 1), *ghost(half), None, q_refs, f_refs)
    turn_sources(0, False, True, q_refs, qs_b)
    convert_features(False, True, None, f_refs, f_b)
    speed = pair_sums(QK, mid, own[3:6], own[6:9], pairs, pair_row, count, ends_ref, mob_ref, *tables)
    best = jnp.max(dot3(speed, speed), axis=0, keepdims=True)
    waiting = []

    def spread(stage, value):
        base = sum(len(line) for line in lines[:stage])
        mid_ref[stage] = value
        sent = [
            remote(mid_ref.at[stage], box_ref.at[base + o], ms.at[base + o], mr.at[base + o], peer)
            for o, peer in enumerate(lines[stage])
        ]
        for copy in sent:
            copy.start()
        waiting.extend(sent)
        return base, sent

    def settle(state, value):
        base, sent = state
        for copy in sent:
            copy.wait_recv()
        for o in range(len(sent)):
            value = jnp.maximum(value, box_ref[base + o])
        return value

    state = spread(0, best)
    for c in range(3):
        v_ref[c] = speed[c]
    best = settle(state, best)
    state = spread(1, best)
    first, second = gather_ends(v_ref, [ends_ref[0], ends_ref[1]])
    rows = [0.5 * (first[c] + second[c]) for c in range(3)] + [second[c] - first[c] for c in range(3)]
    for c in range(6):
        own_v_ref[c] = rows[c]
        for k in range(BLK):
            block_ref[k, c : c + 1, :] = rows[c][k : k + 1]
    pack_blocks(send_list, block_ref, 6, send_v_ref)
    copies_v = ghost_copies(send_v_ref, recv_v_ref, gs2, gr2, targets)
    for copy in copies_v:
        copy.start()
    best = settle(state, best)
    state = spread(2, best)
    own = [own_ref[c] for c in range(9)]
    mid = [own[c] - centre[c] for c in range(3)]
    own_v = [own_v_ref[c] for c in range(6)]
    spread_features(1, 0, mid, own[3:6], own[6:9], (own_v[0:3], own_v[3:6]), q_refs, f_refs)
    turn_sources(1, True, False, q_refs, qs_b)
    for copy in copies_v:
        copy.wait_recv()
    for c in range(6):
        for k in range(8):
            ghost_v_ref[c, 8 * k : 8 * k + GB, :] = recv_v_ref[k, pl.ds(c, GB, stride=6), :]
    for half in range(2):
        moving = [ghost_v_ref[c, BLK * half : BLK * (half + 1), :] for c in range(6)]
        spread_features(1, BLK * (half + 1), *ghost(half), (moving[0:3], moving[3:6]), q_refs, f_refs)
    turn_sources(1, False, True, q_refs, qs_b)
    best = settle(state, best)
    step = DX_LIMIT / (jnp.sqrt(jnp.max(best)) + SPEED_EPS)
    convert_features(True, True, step, f_refs, f_b)
    mid = [mid[c] + step * own_v[c] for c in range(3)]
    line = [own[3 + c] + step * own_v[3 + c] for c in range(3)]
    convert_targets(mid, step, t_refs, qt_b)
    speed = pair_sums(2 * QK, mid, line, own[6:9], pairs, pair_row, count, ends_ref, mob_ref, *tables)
    for c in range(3):
        stage_ref[pl.ds(c, BLK, stride=8), :] = 0.5 * step * (v_ref[c] + speed[c])
    for k in range(BLK):
        out_ref[:, pl.ds(k * LANE, LANE)] = stage_ref[8 * k : 8 * k + 3, :]
    for copy in copies + copies_v + waiting:
        copy.wait_send()


VMEM = pl.BlockSpec(memory_space=pltpu.VMEM)
HBM = pl.BlockSpec(memory_space=pltpu.HBM)
DMA = pltpu.SemaphoreType.DMA


def local(nodes, links, burgers, mobility, send_list, pair_list, pair_count):
    n_gx = lax.axis_size("gx")
    n_yz = lax.axis_size("yz")
    stages = STAGES
    mail = sum(math.prod(size for _, _, size in stage) - 1 for stage in stages)
    scratch = [
        pltpu.VMEM((3, BLK * LANE), F32),
        pltpu.VMEM((2, BLK * LANE), jnp.int32),
        pltpu.VMEM((3, BLK * LANE), F32),
        pltpu.VMEM((3, 3, BLK * LANE), F32),
        pltpu.SMEM((GB, 1, 8), jnp.int32),
        pltpu.SMEM((2, PAIRS), jnp.int32),
        pltpu.SMEM((1,), jnp.int32),
        pltpu.VMEM((2, PAIRS), jnp.int32),
        DMA((8,)),
        pltpu.VMEM((9, BLK, LANE), F32),
        pltpu.VMEM((6, BLK, LANE), F32),
        pltpu.VMEM((3, BLK, LANE), F32),
        pltpu.VMEM((2, BLK, LANE), jnp.int32),
        pltpu.VMEM((9, BLK, LANE), F32),
        pltpu.VMEM((9, 64, LANE), F32),
        pltpu.VMEM((6, 64, LANE), F32),
        pltpu.VMEM((BLK * 8, LANE), F32),
        pltpu.VMEM((BLK, 16, LANE), F32),
        pltpu.VMEM((8, 9 * GB, LANE), F32),
        pltpu.VMEM((8, 9 * GB, LANE), F32),
        pltpu.VMEM((8, 6 * GB, LANE), F32),
        pltpu.VMEM((8, 6 * GB, LANE), F32),
        pltpu.VMEM((mail, 1, LANE), F32),
        pltpu.VMEM((len(stages), 1, LANE), F32),
        DMA((8,)), DMA((8,)), DMA((8,)), DMA((8,)), DMA((mail,)), DMA((mail,)),
        *[pltpu.VMEM((SLOTS * QRAW, LANE), F32)] * 2,
        *[pltpu.VMEM((SLOTS * FRAW, LANE), F32)] * 3,
        *[pltpu.VMEM((BLK * QRAW, LANE), F32)] * 2,
        pltpu.VMEM((SLOTS, LANE, 2 * QK), BF16),
        pltpu.VMEM((BLK, 2 * QK, LANE), BF16),
        pltpu.VMEM((SLOTS, 2 * FRAW, 2 * LANE), BF16),
        pltpu.VMEM((FRAW * PSTRIDE, LANE), F32),
        pltpu.VMEM((6, BLK, LANE), F32),
    ]
    return pl.pallas_call(
        functools.partial(step_kernel, stages),
        out_shape=pltpu.VMEM((3, BLK * LANE), F32),
        in_specs=[HBM] * 7,
        out_specs=VMEM,
        scratch_shapes=scratch,
        compiler_params=pltpu.CompilerParams(collective_id=0, has_side_effects=True, vmem_limit_bytes=56 * 1024 * 1024),
        name="step",
    )(jnp.transpose(send_list, (2, 0, 1)), pair_list, pair_count, nodes, links, burgers, mobility)


def solution(mesh):
    return jax.shard_map(
        local,
        mesh=mesh,
        in_specs=(
            P(None, ("gx", "yz")),
            P(None, ("gx", "yz")),
            P(None, ("gx", "yz")),
            P(None, None, ("gx", "yz")),
            P(("gx", "yz"), None, None),
            P(None, ("gx", "yz")),
            P(("gx", "yz")),
        ),
        out_specs=P(None, ("gx", "yz")),
        check_vma=False,
    )
```

```python
import functools
import itertools
import math

import jax
import jax.numpy as jnp
from jax import lax
from jax.experimental import pallas as pl
from jax.experimental.pallas import tpu as pltpu
from jax.sharding import PartitionSpec as P

F32 = jnp.float32
BF16 = jnp.bfloat16
A_SQUARED = 0.25
NU_FACTOR = 0.4
DX_LIMIT = 1.0
SPEED_EPS = 1e-05
DIRECTIONS = ((-1, -1), (-1, 0), (-1, 1), (0, -1), (0, 1), (1, -1), (1, 0), (1, 1))
BLK = 32
LANE = 128
GB = 6
SLOTS = BLK + 64
QRAW = 8
FRAW = 24
CONV = 16
GTRIP = 2
QK = 6 * QRAW
UNROLL = 40
SCAT = 16
PAIRS = 160
PSTRIDE = PAIRS + 8
MESH_ID = pl.DeviceIdType.MESH
STAGES = ((("yz", 1, 2),), (("gx", 1, 4), ("yz", 2, 4)), (("gx", 4, 4), ("yz", 8, 4)))


def cross(u, v):
    return [u[1] * v[2] - u[2] * v[1], u[2] * v[0] - u[0] * v[2], u[0] * v[1] - u[1] * v[0]]


def dot3(u, v):
    return u[0] * v[0] + u[1] * v[1] + u[2] * v[2]


def rounded(x):
    return x.astype(BF16).astype(F32)


def split2(x):
    high = rounded(x)
    return high, rounded(x - high)


def split3(x):
    high = rounded(x)
    rest = x - high
    mid = rounded(rest)
    return high, mid, rounded(rest - mid)


def to_rows(src_ref, rows, stage_ref, lead=None):
    for k in range(BLK):
        lanes = pl.ds(k * LANE, LANE)
        piece = src_ref[:, lanes] if lead is None else src_ref[lead, :, lanes]
        stage_ref[8 * k : 8 * k + rows, :] = piece
    return [stage_ref[pl.ds(c, BLK, stride=8), :] for c in range(rows)]


def gather_ends(table_ref, ends):
    outs = []
    for end in ends:
        high = end >> 7
        low = end & 127

        def rows_step(step, picked, high=high, low=low):
            picked = list(picked)
            for j in range(8):
                row = 8 * step + j
                here = high == row
                for c in range(3):
                    wide = jnp.broadcast_to(table_ref[c, pl.ds(row, 1), :], (BLK, LANE))
                    found = jnp.take_along_axis(wide, low, axis=1, mode="promise_in_bounds")
                    picked[c] = jnp.where(here, found, picked[c])
            return tuple(picked)

        picked = lax.fori_loop(0, BLK // 8, rows_step, tuple(jnp.zeros((BLK, LANE), F32) for _ in range(3)))
        outs.append(picked)
    return outs


def pack_blocks(send_list, block_ref, rows, send_ref):
    for k in range(8):
        for g in range(GB):
            chosen = send_list[g, 0, k]
            send_ref[k, rows * g : rows * (g + 1), :] = block_ref[chosen, 0:rows, :]


def digits(stage):
    place = {"gx": lax.axis_index("gx"), "yz": lax.axis_index("yz")}
    found = []
    for offsets in itertools.product(*[range(size) for _, _, size in stage]):
        if any(offsets):
            peer = dict(place)
            for (axis, stride, size), offset in zip(stage, offsets):
                digit = lax.rem(lax.div(place[axis], stride), size)
                peer[axis] = peer[axis] + (lax.rem(digit + offset, size) - digit) * stride
            found.append((peer["gx"], peer["yz"]))
    return found


def neighbours():
    gx = lax.axis_index("gx")
    yz = lax.axis_index("yz")
    n_gx = lax.axis_size("gx")
    n_yz = lax.axis_size("yz")
    return [(lax.rem(gx + dx + n_gx, n_gx), lax.rem(yz + dy + n_yz, n_yz)) for dx, dy in DIRECTIONS]


def remote(source, target, send_sem, recv_sem, device):
    return pltpu.make_async_remote_copy(
        src_ref=source, dst_ref=target, send_sem=send_sem, recv_sem=recv_sem, device_id=device, device_id_type=MESH_ID
    )


def ghost_copies(send_ref, recv_ref, send_sem, recv_sem, targets):
    return [remote(send_ref.at[k], recv_ref.at[k], send_sem.at[k], recv_sem.at[k], targets[k]) for k in range(8)]


def put_rows(ref, slot, height, values):
    for row, value in enumerate(values):
        if value is not None:
            ref[pl.ds(slot * height + row, BLK, stride=height), :] = value


def filled(value):
    return jnp.full((BLK, LANE), value, F32)


def spread_features(order, slot, mid, line, burg, slope, q_refs, f_refs):
    moment = cross(burg, mid)
    if order == 0:
        put_rows(q_refs[0], slot, QRAW, mid + [dot3(mid, mid) + A_SQUARED, filled(1.0)] + [filled(0.0)] * 3)
        put_rows(f_refs[0], slot, FRAW, [line[a] * burg[d] for a in range(3) for d in range(3)])
        put_rows(f_refs[0], slot, FRAW, [None] * 9 + [line[a] * moment[d] for a in range(3) for d in range(3)])
        return
    mid_v, line_v = slope
    moment_v = cross(burg, mid_v)
    put_rows(q_refs[1], slot, QRAW, mid_v + [2.0 * dot3(mid, mid_v), dot3(mid_v, mid_v)] + [filled(0.0)] * 3)
    put_rows(f_refs[1], slot, FRAW, [line_v[a] * burg[d] for a in range(3) for d in range(3)])
    put_rows(
        f_refs[1], slot, FRAW,
        [None] * 9 + [line[a] * moment_v[d] + line_v[a] * moment[d] for a in range(3) for d in range(3)],
    )
    put_rows(f_refs[2], slot, FRAW, [filled(0.0)] * 9 + [line_v[a] * moment_v[d] for a in range(3) for d in range(3)])


def over_slots(own, ghosts, body):
    def own_trip(trip, carry):
        for j in range(CONV):
            body(CONV * trip + j)
        return carry

    def ghost_trip(trip, carry):
        for j in range(8 * GTRIP):
            if j % 8 < GB:
                body(BLK + 8 * GTRIP * trip + j)
        return carry

    if own:
        lax.fori_loop(0, BLK // CONV, own_trip, 0)
    if ghosts:
        lax.fori_loop(0, 8 // GTRIP, ghost_trip, 0)


def turn_sources(order, own, ghosts, q_refs, qs_b):
    def body(slot):
        rows = pl.ds(pl.multiple_of(slot * QRAW, 8), QRAW)
        high, mid, low = split3(q_refs[order][rows, :])
        turned = jnp.transpose(jnp.concatenate([high, high, mid, mid, high, low], axis=0).astype(BF16))
        qs_b[slot, :, QK * order : QK * (order + 1)] = turned

    over_slots(own, ghosts, body)


def convert_features(own, ghosts, step, f_refs, f_b):
    def body(slot):
        rows = pl.ds(pl.multiple_of(slot * FRAW, 8), FRAW)
        value = f_refs[0][rows, :]
        if step is not None:
            value = value + step * (f_refs[1][rows, :] + step * f_refs[2][rows, :])
        high, low = split2(value)
        part = jnp.concatenate([high, low], axis=0).astype(BF16)
        f_b[slot, :, 0:LANE] = part
        f_b[slot, :, LANE : 2 * LANE] = part

    over_slots(own, ghosts, body)


def convert_targets(mid, step, t_refs, qt_b):
    put_rows(t_refs[0], 0, QRAW, [-2.0 * mid[c] for c in range(3)] + [filled(1.0), dot3(mid, mid)] + [filled(0.0)] * 3)
    orders = 1
    if step is not None:
        orders = 2
        flat = filled(1.0) * step
        put_rows(t_refs[1], 0, QRAW, [-2.0 * step * mid[c] for c in range(3)] + [flat, step * flat] + [filled(0.0)] * 3)

    def body(trip, carry):
        for j in range(CONV):
            slot = CONV * trip + j
            for order in range(orders):
                high, mid_part, low = split3(t_refs[order][pl.ds(pl.multiple_of(slot * QRAW, 8), QRAW), :])
                qt_b[slot, QK * order : QK * (order + 1), :] = jnp.concatenate(
                    [high, mid_part, high, mid_part, low, high], axis=0
                ).astype(BF16)
        return carry

    lax.fori_loop(0, BLK // CONV, body, 0)


def pair_sums(depth, mid, line, burg, pairs, pair_row, count, ends_ref, mob_ref, qs_b, qt_b, f_b, acc, force_ref):
    def pair_step(step, carry):
        for j in range(UNROLL):
            place = UNROLL * step + j
            target = jnp.minimum(pairs[0, place], BLK - 1)
            source = pairs[1, place]
            ghost_place = source - BLK
            group = (ghost_place * 43) >> 8
            slot = jnp.where(source < BLK, source, BLK + 8 * group + (ghost_place - GB * group))
            dist = jnp.dot(qs_b[slot, :, 0:depth], qt_b[target, 0:depth, :], preferred_element_type=F32)
            root = lax.rsqrt(dist)
            weight = root * root * root
            high = weight.astype(BF16)
            low = (weight - high.astype(F32)).astype(BF16)
            both = jnp.concatenate([high, low], axis=0)
            found = jnp.dot(f_b[slot], both, preferred_element_type=F32)
            acc[pl.ds(place, FRAW, stride=PSTRIDE), :] = found[0:FRAW] + found[FRAW : 2 * FRAW]
        return carry

    lax.fori_loop(0, PAIRS // UNROLL, pair_step, 0)
    pair_id = lax.broadcasted_iota(jnp.int32, (BLK, PAIRS), 1)
    block_id = lax.broadcasted_iota(jnp.int32, (BLK, PAIRS), 0)
    chosen = jnp.where((block_id == pair_row[0:1, :]) & (pair_id < count), 1.0, 0.0).astype(BF16)
    chosen = jnp.concatenate([chosen, chosen], axis=1)

    def total(row):
        part = acc[PSTRIDE * row : PSTRIDE * row + PAIRS, :]
        high = part.astype(BF16)
        low = (part - high.astype(F32)).astype(BF16)
        return jnp.dot(chosen, jnp.concatenate([high, low], axis=0), preferred_element_type=F32)

    s_mat = [[total(3 * a + d) for d in range(3)] for a in range(3)]
    t_mat = [[total(9 + 3 * a + d) for d in range(3)] for a in range(3)]
    arm = cross(mid, burg)
    lined_s = [burg[0] * s_mat[0][d] + burg[1] * s_mat[1][d] + burg[2] * s_mat[2][d] for d in range(3)]
    lined_t = [burg[0] * t_mat[0][d] + burg[1] * t_mat[1][d] + burg[2] * t_mat[2][d] for d in range(3)]
    swept = cross(lined_s, mid)
    skew = [s_mat[2][1] - s_mat[1][2], s_mat[0][2] - s_mat[2][0], s_mat[1][0] - s_mat[0][1]]
    twist = NU_FACTOR * (dot3(mid, skew) + (t_mat[0][0] + t_mat[1][1] + t_mat[2][2]))
    traction = [
        0.5 * ((dot3(s_mat[k], arm) - dot3(t_mat[k], burg)) + (swept[k] - lined_t[k])) + twist * burg[k]
        for k in range(3)
    ]
    force = cross(traction, line)
    for c in range(3):
        high, low = split2(0.5 * force[c])
        force_ref[2 * c] = high
        force_ref[2 * c + 1] = low

    row_id = lax.broadcasted_iota(jnp.int32, (BLK, LANE), 0)
    lane_id = lax.broadcasted_iota(jnp.int32, (LANE, LANE), 0)

    def scatter_step(step, nodal):
        lhs = []
        rhs = []
        for j in range(SCAT):
            k = SCAT * step + j
            for e in range(2):
                end = ends_ref[e, pl.ds(k, 1), :]
                here = row_id == (end >> 7)
                lhs.append(
                    jnp.concatenate(
                        [jnp.where(here, force_ref[i, pl.ds(k, 1), :], 0.0).astype(BF16) for i in range(6)], axis=0
                    )
                )
                rhs.append(jnp.where(lane_id == (end & 127), 1.0, 0.0).astype(BF16))
        return nodal + lax.dot_general(
            jnp.concatenate(lhs, axis=1),
            jnp.concatenate(rhs, axis=1),
            (((1,), (1,)), ((), ())),
            preferred_element_type=F32,
        )

    nodal = lax.fori_loop(0, BLK // SCAT, scatter_step, jnp.zeros((6 * BLK, LANE), F32))
    pulled = [nodal[2 * BLK * c : 2 * BLK * c + BLK] + nodal[2 * BLK * c + BLK : 2 * BLK * (c + 1)] for c in range(3)]
    return [dot3([mob_ref[3 * r + c] for c in range(3)], pulled) for r in range(3)]


def step_kernel(
    stages, send_list_hbm, pairs_hbm, count_hbm, nodes_hbm, links_hbm, burgers_hbm, mobility_hbm, out_ref,
    nodes_ref, links_ref, burgers_ref, mobility_ref, send_list, pairs, count_ref, pair_row, in_sem,
    own_ref, own_v_ref, v_ref, ends_ref, mob_ref, ghost_ref, ghost_v_ref, stage_ref, block_ref,
    send_ref, recv_ref, send_v_ref, recv_v_ref, box_ref, mid_ref, gs1, gr1, gs2, gr2, ms, mr,
    q0_ref, q1_ref, f0_ref, f1_ref, f2_ref, t0_ref, t1_ref, qs_b, qt_b, f_b, acc, force_ref
):
    loads = [
        pltpu.make_async_copy(src, dst, in_sem.at[i])
        for i, (src, dst) in enumerate(
            (
                (nodes_hbm, nodes_ref),
                (links_hbm, links_ref),
                (burgers_hbm, burgers_ref),
                (send_list_hbm, send_list),
                (mobility_hbm, mobility_ref),
                (pairs_hbm, pairs),
                (pairs_hbm, pair_row),
                (count_hbm, count_ref),
            )
        )
    ]
    for load in loads:
        load.start()
    targets = neighbours()
    lines = [digits(stage) for stage in stages]
    peers = targets + [peer for line in lines for peer in line]
    barrier = pltpu.get_barrier_semaphore()
    for peer in peers:
        pl.semaphore_signal(barrier, inc=1, device_id=peer, device_id_type=MESH_ID)

    loads[0].wait()
    coords = to_rows(nodes_ref, 3, stage_ref)
    for c in range(3):
        v_ref[c] = coords[c]
    loads[1].wait()
    for k in range(BLK):
        lanes = pl.ds(k * LANE, LANE)
        ends_ref[0, k : k + 1, :] = links_ref[0:1, lanes]
        ends_ref[1, k : k + 1, :] = links_ref[1:2, lanes]
    first, second = gather_ends(v_ref, [ends_ref[0], ends_ref[1]])
    loads[2].wait()
    rows = [0.5 * (first[c] + second[c]) for c in range(3)] + [second[c] - first[c] for c in range(3)]
    rows = rows + to_rows(burgers_ref, 3, stage_ref)
    for c in range(9):
        own_ref[c] = rows[c]
        for k in range(BLK):
            block_ref[k, c : c + 1, :] = rows[c][k : k + 1]
    loads[3].wait()
    pack_blocks(send_list, block_ref, 9, send_ref)
    pl.semaphore_wait(barrier, len(peers))
    copies = ghost_copies(send_ref, recv_ref, gs1, gr1, targets)
    for copy in copies:
        copy.start()
    for load in loads[4:]:
        load.wait()
    count = count_ref[0]
    for r in range(3):
        rows = to_rows(mobility_ref, 3, stage_ref, r)
        for c in range(3):
            mob_ref[3 * r + c] = rows[c]

    q_refs = (q0_ref, q1_ref)
    t_refs = (t0_ref, t1_ref)
    f_refs = (f0_ref, f1_ref, f2_ref)
    tables = (qs_b, qt_b, f_b, acc, force_ref)
    own = [own_ref[c] for c in range(9)]
    centre = [jnp.mean(own[c]) for c in range(3)]
    mid = [own[c] - centre[c] for c in range(3)]
    spread_features(0, 0, mid, own[3:6], own[6:9], None, q_refs, f_refs)
    turn_sources(0, True, False, q_refs, qs_b)
    convert_features(True, False, None, f_refs, f_b)
    convert_targets(mid, None, t_refs, qt_b)
    for copy in copies:
        copy.wait_recv()
    for c in range(9):
        for k in range(8):
            ghost_ref[c, 8 * k : 8 * k + GB, :] = recv_ref[k, pl.ds(c, GB, stride=9), :]
            ghost_ref[c, 8 * k + GB : 8 * k + 8, :] = jnp.zeros((8 - GB, LANE), F32)
            if c < 6:
                ghost_v_ref[c, 8 * k + GB : 8 * k + 8, :] = jnp.zeros((8 - GB, LANE), F32)

    def ghost(half):
        rows = [ghost_ref[c, BLK * half : BLK * (half + 1), :] for c in range(9)]
        return [rows[c] - centre[c] for c in range(3)], rows[3:6], rows[6:9]

    for half in range(2):
        spread_features(0, BLK * (half + 1), *ghost(half), None, q_refs, f_refs)
    turn_sources(0, False, True, q_refs, qs_b)
    convert_features(False, True, None, f_refs, f_b)
    speed = pair_sums(QK, mid, own[3:6], own[6:9], pairs, pair_row, count, ends_ref, mob_ref, *tables)
    best = jnp.max(dot3(speed, speed), axis=0, keepdims=True)
    waiting = []

    def spread(stage, value):
        base = sum(len(line) for line in lines[:stage])
        mid_ref[stage] = value
        sent = [
            remote(mid_ref.at[stage], box_ref.at[base + o], ms.at[base + o], mr.at[base + o], peer)
            for o, peer in enumerate(lines[stage])
        ]
        for copy in sent:
            copy.start()
        waiting.extend(sent)
        return base, sent

    def settle(state, value):
        base, sent = state
        for copy in sent:
            copy.wait_recv()
        for o in range(len(sent)):
            value = jnp.maximum(value, box_ref[base + o])
        return value

    state = spread(0, best)
    for c in range(3):
        v_ref[c] = speed[c]
    best = settle(state, best)
    state = spread(1, best)
    first, second = gather_ends(v_ref, [ends_ref[0], ends_ref[1]])
    rows = [0.5 * (first[c] + second[c]) for c in range(3)] + [second[c] - first[c] for c in range(3)]
    for c in range(6):
        own_v_ref[c] = rows[c]
        for k in range(BLK):
            block_ref[k, c : c + 1, :] = rows[c][k : k + 1]
    pack_blocks(send_list, block_ref, 6, send_v_ref)
    copies_v = ghost_copies(send_v_ref, recv_v_ref, gs2, gr2, targets)
    for copy in copies_v:
        copy.start()
    best = settle(state, best)
    state = spread(2, best)
    own = [own_ref[c] for c in range(9)]
    mid = [own[c] - centre[c] for c in range(3)]
    own_v = [own_v_ref[c] for c in range(6)]
    spread_features(1, 0, mid, own[3:6], own[6:9], (own_v[0:3], own_v[3:6]), q_refs, f_refs)
    turn_sources(1, True, False, q_refs, qs_b)
    for copy in copies_v:
        copy.wait_recv()
    for c in range(6):
        for k in range(8):
            ghost_v_ref[c, 8 * k : 8 * k + GB, :] = recv_v_ref[k, pl.ds(c, GB, stride=6), :]
    for half in range(2):
        moving = [ghost_v_ref[c, BLK * half : BLK * (half + 1), :] for c in range(6)]
        spread_features(1, BLK * (half + 1), *ghost(half), (moving[0:3], moving[3:6]), q_refs, f_refs)
    turn_sources(1, False, True, q_refs, qs_b)
    best = settle(state, best)
    step = DX_LIMIT / (jnp.sqrt(jnp.max(best)) + SPEED_EPS)
    convert_features(True, True, step, f_refs, f_b)
    mid = [mid[c] + step * own_v[c] for c in range(3)]
    line = [own[3 + c] + step * own_v[3 + c] for c in range(3)]
    convert_targets(mid, step, t_refs, qt_b)
    speed = pair_sums(2 * QK, mid, line, own[6:9], pairs, pair_row, count, ends_ref, mob_ref, *tables)
    for c in range(3):
        stage_ref[pl.ds(c, BLK, stride=8), :] = 0.5 * step * (v_ref[c] + speed[c])
    for k in range(BLK):
        out_ref[:, pl.ds(k * LANE, LANE)] = stage_ref[8 * k : 8 * k + 3, :]
    for copy in copies + copies_v + waiting:
        copy.wait_send()


VMEM = pl.BlockSpec(memory_space=pltpu.VMEM)
HBM = pl.BlockSpec(memory_space=pltpu.HBM)
DMA = pltpu.SemaphoreType.DMA


def local(nodes, links, burgers, mobility, send_list, pair_list, pair_count):
    n_gx = lax.axis_size("gx")
    n_yz = lax.axis_size("yz")
    stages = STAGES
    mail = sum(math.prod(size for _, _, size in stage) - 1 for stage in stages)
    scratch = [
        pltpu.VMEM((3, BLK * LANE), F32),
        pltpu.VMEM((2, BLK * LANE), jnp.int32),
        pltpu.VMEM((3, BLK * LANE), F32),
        pltpu.VMEM((3, 3, BLK * LANE), F32),
        pltpu.SMEM((GB, 1, 8), jnp.int32),
        pltpu.SMEM((2, PAIRS), jnp.int32),
        pltpu.SMEM((1,), jnp.int32),
        pltpu.VMEM((2, PAIRS), jnp.int32),
        DMA((8,)),
        pltpu.VMEM((9, BLK, LANE), F32),
        pltpu.VMEM((6, BLK, LANE), F32),
        pltpu.VMEM((3, BLK, LANE), F32),
        pltpu.VMEM((2, BLK, LANE), jnp.int32),
        pltpu.VMEM((9, BLK, LANE), F32),
        pltpu.VMEM((9, 64, LANE), F32),
        pltpu.VMEM((6, 64, LANE), F32),
        pltpu.VMEM((BLK * 8, LANE), F32),
        pltpu.VMEM((BLK, 16, LANE), F32),
        pltpu.VMEM((8, 9 * GB, LANE), F32),
        pltpu.VMEM((8, 9 * GB, LANE), F32),
        pltpu.VMEM((8, 6 * GB, LANE), F32),
        pltpu.VMEM((8, 6 * GB, LANE), F32),
        pltpu.VMEM((mail, 1, LANE), F32),
        pltpu.VMEM((len(stages), 1, LANE), F32),
        DMA((8,)), DMA((8,)), DMA((8,)), DMA((8,)), DMA((mail,)), DMA((mail,)),
        *[pltpu.VMEM((SLOTS * QRAW, LANE), F32)] * 2,
        *[pltpu.VMEM((SLOTS * FRAW, LANE), F32)] * 3,
        *[pltpu.VMEM((BLK * QRAW, LANE), F32)] * 2,
        pltpu.VMEM((SLOTS, LANE, 2 * QK), BF16),
        pltpu.VMEM((BLK, 2 * QK, LANE), BF16),
        pltpu.VMEM((SLOTS, 2 * FRAW, 2 * LANE), BF16),
        pltpu.VMEM((FRAW * PSTRIDE, LANE), F32),
        pltpu.VMEM((6, BLK, LANE), F32),
    ]
    return pl.pallas_call(
        functools.partial(step_kernel, stages),
        out_shape=pltpu.VMEM((3, BLK * LANE), F32),
        in_specs=[HBM] * 7,
        out_specs=VMEM,
        scratch_shapes=scratch,
        compiler_params=pltpu.CompilerParams(collective_id=0, has_side_effects=True, vmem_limit_bytes=56 * 1024 * 1024),
        name="step",
    )(jnp.transpose(send_list, (2, 0, 1)), pair_list, pair_count, nodes, links, burgers, mobility)


def solution(mesh):
    return jax.shard_map(
        local,
        mesh=mesh,
        in_specs=(
            P(None, ("gx", "yz")),
            P(None, ("gx", "yz")),
            P(None, ("gx", "yz")),
            P(None, None, ("gx", "yz")),
            P(("gx", "yz"), None, None),
            P(None, ("gx", "yz")),
            P(("gx", "yz")),
        ),
        out_specs=P(None, ("gx", "yz")),
        check_vma=False,
    )
```
